32 devices in a mesh: ctx: 8 (over y, x, core), head: 4 (over z).
Axes of the slice: x: 2, y: 2, z: 4, core: 2. Of those that a mesh axis runs over, the one named last changes fastest.
Arguments:
- routed_q: bfloat16 [4096, 1024], P('ctx', 'head'), may hold values from -16 to 16
- routed_k: bfloat16 [4096, 1024], P('ctx', 'head'), may hold values from -16 to 16
- routed_v: bfloat16 [4096, 1024], P('ctx', 'head'), may hold values from -6 to 6
- routed_grad: bfloat16 [4096, 1024], P('ctx', 'head'), may hold values from -6 to 6
- local_q: bfloat16 [4096, 1024], P('ctx', 'head'), may hold values from -16 to 16
- local_k: bfloat16 [4096, 1024], P('ctx', 'head'), may hold values from -16 to 16
- local_v: bfloat16 [4096, 1024], P('ctx', 'head'), may hold values from -6 to 6
- local_grad: bfloat16 [4096, 1024], P('ctx', 'head'), may hold values from -6 to 6
- clusters: int32 [8, 4096], P('head', 'ctx'), may hold values from 0 to 63, as said below
- cluster_slot: int32 [8, 64], P('head'), may hold values from 0 to 63, each once within a row
- rel_bias: float32 [128], replicated, may hold values from -4 to 4
Outputs:
- routed_out: bfloat16 [4096, 1024], P('ctx', 'head')
- routed_dq: bfloat16 [4096, 1024], P('ctx', 'head')
- routed_dk: bfloat16 [4096, 1024], P('ctx', 'head')
- routed_dv: bfloat16 [4096, 1024], P('ctx', 'head')
- centroids: float32 [8, 64, 128], P('head', 'ctx')
- local_out: bfloat16 [4096, 1024], P('ctx', 'head')
- local_dq: bfloat16 [4096, 1024], P('ctx', 'head')
- local_dk: bfloat16 [4096, 1024], P('ctx', 'head')
- local_dv: bfloat16 [4096, 1024], P('ctx', 'head')
- bias_grad: float32 [128], replicated
The draws below stay inside these ranges and needn't reach their ends.
Inputs may be any that keep to these rules, and one draw needn't show every extreme that they name: `clusters`: among the 512 positions of one index of ctx, at most 16 name the same cluster for one routed head; for every routed head one cluster is named exactly 16 times on every index of ctx.
All inputs are finite; a program needn't handle non-finite values.
Results may differ from the reference program's by a relative error of at most 0.0077.
Values may be sent and summed in bfloat16 or wider, within the bound.
No kernel may reach another device: no remote copies, remote signals or barrier semaphores. Data moves between devices by JAX's collectives and lax.ppermute only.
A program may use at most 64 MiB of HBM per device.

```python
import jax
import jax.numpy as jnp
from jax import lax

HEAD_DIM = 128
ROUTED_HEADS = 8
LOCAL_HEADS = 8
WINDOW = 128
TOK_DEV = 512
SEQUENCE = 4096
CLUST_DEV = 8
CLUSTERS = 64
PER_SOURCE = 16
CAPACITY = 128
N_CTX = 8


def cluster_table(key):
    device_count = SEQUENCE // TOK_DEV
    pair_count = CLUSTERS // 2
    base_key = jax.random.fold_in(key, 7)
    key_division, key_labels, key_orders = jax.random.split(base_key, 3)
    division = jax.random.randint(key_division, (ROUTED_HEADS, device_count, pair_count), 0, PER_SOURCE + 1)
    division = division.at[:, :, 0].set(PER_SOURCE)
    position = jnp.arange(TOK_DEV, dtype=jnp.int32)
    pair_index = position // PER_SOURCE
    within = position % PER_SOURCE
    chosen = division[:, :, pair_index]
    labels = 2 * pair_index[None, None, :] + (within[None, None, :] >= chosen).astype(jnp.int32)
    relabel = jax.vmap(lambda sub_key: jax.random.permutation(sub_key, CLUSTERS))(jax.random.split(key_labels, ROUTED_HEADS)).astype(jnp.int32)
    labels = jax.vmap(lambda table, entries: table[entries])(relabel, labels)
    orders = jax.vmap(lambda sub_key: jax.random.permutation(sub_key, TOK_DEV))(jax.random.split(key_orders, ROUTED_HEADS * device_count))
    orders = orders.reshape(ROUTED_HEADS, device_count, TOK_DEV).astype(jnp.int32)
    labels = jnp.take_along_axis(labels, orders, axis=2)
    return labels.reshape(ROUTED_HEADS, SEQUENCE).astype(jnp.int32)


def routed_pair(key, which):
    gaussian = jax.random.truncated_normal(jax.random.fold_in(key, 20 + which), -6.0, 6.0, (SEQUENCE, ROUTED_HEADS, HEAD_DIM))
    return gaussian.reshape(SEQUENCE, ROUTED_HEADS * HEAD_DIM).astype(jnp.bfloat16)


def local_pair(key, which):
    gaussian = jax.random.truncated_normal(jax.random.fold_in(key, 40 + which), -6.0, 6.0, (SEQUENCE, LOCAL_HEADS, HEAD_DIM))
    return gaussian.reshape(SEQUENCE, LOCAL_HEADS * HEAD_DIM).astype(jnp.bfloat16)


def draw_routed_q(key, part):
    return routed_pair(key, 0)


def draw_routed_k(key, part):
    return routed_pair(key, 1)


def draw_local_q(key, part):
    return local_pair(key, 0)


def draw_local_k(key, part):
    return local_pair(key, 1)


def draw_clusters(key, part):
    return cluster_table(key)


def steps_of(rng, dims, cuts, least, top_value):
    def one(dim, parts):
        draws = jax.random.uniform(jax.random.fold_in(jax.random.fold_in(rng, 6), dim), (parts,), jnp.float32, least / len(cuts), top_value / len(cuts))
        return jnp.repeat(jnp.exp(draws), dims[dim] // parts).reshape((-1,) + (1,) * (len(dims) - dim - 1))

    level = one(*cuts[0])
    for cut in cuts[1:]:
        level = level * one(*cut)
    return level


def scatter_about(stream_key, dims, spread, reach, shards=(), kind=jnp.bfloat16):
    level = steps_of(stream_key, dims, shards, -0.22, 0.18) if shards else 1.0
    values = jax.random.normal(stream_key, dims, jnp.float32) * spread * level
    return jnp.minimum(jnp.maximum(values, -reach), reach).astype(kind)


def setup_inputs(seed: int = 0) -> dict:
    streams_of = jax.random.split(jax.random.key(seed), 12)
    return {
        "routed_q": draw_routed_q(jax.random.fold_in(streams_of[11], 71), 0),
        "routed_k": draw_routed_k(jax.random.fold_in(streams_of[11], 71), 0),
        "routed_v": scatter_about(streams_of[2], (SEQUENCE, ROUTED_HEADS * HEAD_DIM), 1.0, 6.0, ((0, 8), (1, 4))),
        "routed_grad": scatter_about(streams_of[3], (SEQUENCE, ROUTED_HEADS * HEAD_DIM), 1.0, 6.0, ((0, 8), (1, 4))),
        "local_q": draw_local_q(jax.random.fold_in(streams_of[11], 71), 0),
        "local_k": draw_local_k(jax.random.fold_in(streams_of[11], 71), 0),
        "local_v": scatter_about(streams_of[6], (SEQUENCE, LOCAL_HEADS * HEAD_DIM), 1.0, 6.0, ((0, 8), (1, 4))),
        "local_grad": scatter_about(streams_of[7], (SEQUENCE, LOCAL_HEADS * HEAD_DIM), 1.0, 6.0, ((0, 8), (1, 4))),
        "clusters": draw_clusters(jax.random.fold_in(streams_of[11], 71), 0),
        "cluster_slot": jax.vmap(lambda own: jax.random.permutation(own, CLUSTERS))(jax.random.split(streams_of[9], ROUTED_HEADS)).reshape((ROUTED_HEADS, CLUSTERS)).astype(jnp.int32),
        "rel_bias": scatter_about(streams_of[10], (WINDOW,), 1.0, 4.0, (), jnp.float32),
    }


NEG = -1e+30

def softmax_rows(query, keys, allowed, offset_bias):
    scaling = query.shape[-1] ** (-0.5)
    scores = jnp.einsum('bmd,bnd->bmn', query.astype(jnp.float32), keys.astype(jnp.float32)) * scaling + offset_bias
    scores = jnp.where(allowed, scores, NEG)
    row_max = lax.optimization_barrier(jnp.max(scores, axis=-1, keepdims=True))
    exponent = jnp.exp(scores - row_max)
    return exponent / lax.optimization_barrier(jnp.sum(exponent, axis=-1, keepdims=True))

def attend_all(query, keys, values, cotangent, allowed, offset_bias):
    attn_weights = softmax_rows(query, keys, allowed, offset_bias)
    weights_low = lax.optimization_barrier(attn_weights.astype(jnp.bfloat16)).astype(jnp.float32)
    values_wide = values.astype(jnp.float32)
    cot_wide = cotangent.astype(jnp.float32)
    output = jnp.einsum('bmn,bnd->bmd', weights_low, values_wide)
    weight_grad = jnp.einsum('bmd,bnd->bmn', cot_wide, values_wide)
    score_grad = attn_weights * (weight_grad - lax.optimization_barrier(jnp.sum(attn_weights * weight_grad, axis=-1, keepdims=True)))
    score_grad_low = lax.optimization_barrier(score_grad.astype(jnp.bfloat16)).astype(jnp.float32)
    scaling = query.shape[-1] ** (-0.5)
    query_grad = jnp.einsum('bmn,bnd->bmd', score_grad_low, keys.astype(jnp.float32)) * scaling
    keys_grad = jnp.einsum('bmn,bmd->bnd', score_grad_low, query.astype(jnp.float32)) * scaling
    values_grad = jnp.einsum('bmn,bmd->bnd', weights_low, cot_wide)
    return (output, query_grad, keys_grad, values_grad, score_grad)

def offset_table():
    row_index = jnp.arange(WINDOW, dtype=jnp.int32)[:, None]
    col_index = jnp.arange(2 * WINDOW, dtype=jnp.int32)[None, :]
    offset = WINDOW + row_index - col_index
    inside = (offset >= 0) & (offset < WINDOW)
    return (offset, inside)

def routed_head(inputs):
    query, keys, values, cotangent, cluster_ids, slots = inputs
    total = cluster_ids.shape[0]
    head_dim = query.shape[-1]
    sorted_pos = jnp.argsort(cluster_ids, stable=True).astype(jnp.int32)
    sorted_ids = cluster_ids[sorted_pos]
    counts = jnp.zeros((CLUSTERS,), jnp.int32).at[cluster_ids].add(1)
    starts = jnp.cumsum(counts) - counts
    rank_in = jnp.arange(total, dtype=jnp.int32) - starts[sorted_ids]
    destination = jnp.zeros((total,), jnp.int32).at[sorted_pos].set(sorted_ids * CAPACITY + rank_in)

    def pack(array):
        packed = jnp.zeros((CLUSTERS * CAPACITY, head_dim), array.dtype).at[destination].set(array)
        return packed.reshape(CLUST_DEV, N_CTX, CAPACITY, head_dim)
    live_slots = (jnp.arange(CAPACITY, dtype=jnp.int32)[None, :] < counts[:, None]).reshape(CLUST_DEV, N_CTX, CAPACITY)
    causal = jnp.arange(CAPACITY)[:, None] >= jnp.arange(CAPACITY)[None, :]
    diagonal = jnp.eye(CAPACITY, dtype=bool)

    def one_group(group):
        g_query, g_keys, g_values, g_cot, g_live = group
        allowed = g_live[:, None, :] & causal[None] | diagonal[None]
        output, query_grad, keys_grad, values_grad, unused = attend_all(g_query, g_keys, g_values, g_cot, allowed, 0.0)
        return (output.astype(jnp.bfloat16), query_grad.astype(jnp.bfloat16), keys_grad.astype(jnp.bfloat16), values_grad.astype(jnp.bfloat16))
    packed_keys = pack(keys)
    results = lax.map(one_group, (pack(query), packed_keys, pack(values), pack(cotangent), live_slots))
    back = [piece.reshape(CLUSTERS * CAPACITY, head_dim)[destination] for piece in results]
    key_sums = lax.optimization_barrier(jnp.sum(packed_keys.astype(jnp.float32).reshape(CLUSTERS, CAPACITY, head_dim), axis=1))
    normed = key_sums / jnp.sqrt(lax.optimization_barrier(jnp.mean(key_sums * key_sums, axis=-1, keepdims=True)) + 1e-06)
    placed = jnp.zeros_like(normed).at[slots].set(normed)
    return (back[0], back[1], back[2], back[3], placed)

def local_head(inputs, rel_bias):
    query, keys, values, cotangent = inputs
    total, head_dim = query.shape
    block_count = total // WINDOW

    def key_frames(array):
        extended = jnp.concatenate([jnp.zeros((WINDOW, head_dim), array.dtype), array], 0)
        return jnp.concatenate([extended[:-WINDOW].reshape(block_count, WINDOW, head_dim), extended[WINDOW:].reshape(block_count, WINDOW, head_dim)], 1)

    def fold_frames(array):
        earlier_half = array[:, :WINDOW].reshape(total, head_dim)
        later_half = array[:, WINDOW:].reshape(total, head_dim)
        return (jnp.pad(earlier_half, ((0, WINDOW), (0, 0))) + jnp.pad(later_half, ((WINDOW, 0), (0, 0))))[WINDOW:]
    offset, inside = offset_table()
    offset_bias = rel_bias[jnp.clip(offset, 0, WINDOW - 1)]
    key_pos = jnp.arange(block_count, dtype=jnp.int32)[:, None, None] * WINDOW - WINDOW + jnp.arange(2 * WINDOW, dtype=jnp.int32)[None, None, :]
    allowed = inside[None] & (key_pos >= 0)
    output, query_grad, keys_grad, values_grad, score_grad = attend_all(query.reshape(block_count, WINDOW, head_dim), key_frames(keys), key_frames(values), cotangent.reshape(block_count, WINDOW, head_dim), allowed, offset_bias)
    return (output.reshape(total, head_dim).astype(jnp.bfloat16), query_grad.reshape(total, head_dim).astype(jnp.bfloat16), fold_frames(keys_grad).astype(jnp.bfloat16), fold_frames(values_grad).astype(jnp.bfloat16), lax.optimization_barrier(jnp.sum(score_grad, axis=0)))

def reference(routed_q, routed_k, routed_v, routed_grad, local_q, local_k, local_v, local_grad, clusters, cluster_slot, rel_bias):

    def by_head(array):
        return array.reshape(SEQUENCE, -1, HEAD_DIM).transpose(1, 0, 2)

    def merge_heads(array):
        return array.transpose(1, 0, 2).reshape(SEQUENCE, -1)
    routed = lax.map(routed_head, (by_head(routed_q), by_head(routed_k), by_head(routed_v), by_head(routed_grad), clusters, cluster_slot))
    local = lax.map(lambda group: local_head(group, rel_bias), (by_head(local_q), by_head(local_k), by_head(local_v), by_head(local_grad)))
    offset, inside = offset_table()
    segment_ids = jnp.where(inside, offset, WINDOW).reshape(-1)
    bias_grad = jax.ops.segment_sum(lax.optimization_barrier(jnp.sum(local[4], axis=0)).reshape(-1), segment_ids, num_segments=WINDOW + 1)[:WINDOW]
    return (merge_heads(routed[0]), merge_heads(routed[1]), merge_heads(routed[2]), merge_heads(routed[3]), routed[4], merge_heads(local[0]), merge_heads(local[1]), merge_heads(local[2]), merge_heads(local[3]), bias_grad)
```

```python
import jax
import jax.numpy as jnp
from jax import lax
from jax.experimental import pallas as pl
from jax.experimental.pallas import tpu as pltpu
from jax.sharding import PartitionSpec as P

HEAD_DIM = 128
WINDOW = 128

NEG = -1e30
EPSILON = 1e-06
EMPTY = 64.0
EMPTY_LEVEL = 32.0

F32 = jnp.float32
BF16 = jnp.bfloat16


def dot_nn(a, b):
    return lax.dot_general(a, b, (((1,), (0,)), ((), ())), preferred_element_type=F32)


def dot_nt(a, b):
    return lax.dot_general(a, b, (((1,), (1,)), ((), ())), preferred_element_type=F32)


def dot_tn(a, b):
    return lax.dot_general(a, b, (((0,), (0,)), ((), ())), preferred_element_type=F32)


def iota(shape, dim):
    return lax.broadcasted_iota(jnp.int32, shape, dim)


def softmax_and_grads(query, keys, values, cotangent, bias, allowed):
    scaling = query.shape[-1] ** (-0.5)
    scores = dot_nt(query, keys) * scaling
    if bias is not None:
        scores = scores + bias
    scores = jnp.where(allowed, scores, NEG)
    exponent = jnp.exp(scores - jnp.max(scores, axis=-1, keepdims=True))
    probs = exponent * (1.0 / jnp.sum(exponent, axis=-1, keepdims=True))
    dprobs = dot_nt(cotangent, values)
    dscores = probs * (dprobs - jnp.sum(probs * dprobs, axis=-1, keepdims=True))
    return probs, dscores


def pack_kernel(ids_ref, slots_ref, q_ref, k_ref, v_ref, g_ref, out_ref, flat_ref, *, per_source):
    head = pl.program_id(0)
    ids = ids_ref[pl.ds(head, 1), :]
    tokens = ids.shape[1]
    clusters = slots_ref.shape[1]
    dests, _, rows, _ = out_ref.shape
    member = iota((clusters, tokens), 0) == ids
    member_low = jnp.where(member, 1.0, 0.0).astype(BF16)
    earlier = jnp.where(iota((tokens, tokens), 0) < iota((tokens, tokens), 1), 1.0, 0.0).astype(BF16)
    before = dot_nn(member_low, earlier)
    rank = jnp.sum(jnp.where(member, before, 0.0), axis=0, keepdims=True)
    slots = jnp.broadcast_to(slots_ref[pl.ds(head, 1), :], (8, clusters)).astype(F32).astype(BF16)
    flat = dot_nn(slots, member_low)[:1] * per_source + rank
    flat_ref[0] = jnp.broadcast_to(flat, (8, tokens))
    where_to = flat.astype(jnp.int32)
    data = jnp.concatenate([q_ref[...], k_ref[...], v_ref[...], g_ref[...]], axis=1)
    dim = k_ref.shape[1]
    first_col = iota((rows, dim), 1) == 0
    for dest in range(dests):
        chosen = jnp.where(iota((rows, tokens), 0) + dest * rows == where_to, 1.0, 0.0)
        filled = jnp.sum(chosen, axis=1, keepdims=True) > 0.5
        moved = dot_nn(chosen.astype(BF16), data)
        marked = jnp.where(first_col & ~filled, EMPTY, moved[:, dim : 2 * dim])
        out_ref[dest, 0, :, :dim] = moved[:, :dim].astype(BF16)
        out_ref[dest, 0, :, dim : 2 * dim] = marked.astype(BF16)
        out_ref[dest, 0, :, 2 * dim :] = moved[:, 2 * dim :].astype(BF16)


def pack(ids, slots, arrays, dests, per_source):
    tokens = arrays[0].shape[0]
    heads, clusters = slots.shape
    rows = clusters * per_source // dests
    width = len(arrays) * HEAD_DIM
    column = pl.BlockSpec((tokens, HEAD_DIM), lambda h: (0, h))
    return pl.pallas_call(
        lambda *refs: pack_kernel(*refs, per_source=per_source),
        grid=(heads,),
        in_specs=[
            pl.BlockSpec((heads, tokens), lambda h: (0, 0)),
            pl.BlockSpec((heads, clusters), lambda h: (0, 0)),
            column,
            column,
            column,
            column,
        ],
        out_specs=(
            pl.BlockSpec((dests, 1, rows, width), lambda h: (0, h, 0, 0)),
            pl.BlockSpec((1, 8, tokens), lambda h: (h, 0, 0)),
        ),
        out_shape=(
            jax.ShapeDtypeStruct((dests, heads, rows, width), BF16),
            jax.ShapeDtypeStruct((heads, 8, tokens), F32),
        ),
        name="pack",
    )(ids, slots, *arrays)


def owner_kernel(got_ref, out_ref, centroid_ref, *, per_source):
    sources, _, rows, _ = got_ref.shape
    dim = HEAD_DIM
    capacity = sources * per_source
    row = iota((capacity, capacity), 0)
    col = iota((capacity, capacity), 1)
    causal = row >= col
    diagonal = row == col
    pick_first = jnp.where(iota((capacity, dim), 1) == 0, 1.0, 0.0).astype(BF16)
    first_col = iota((capacity, dim), 1) == 0
    scaling = dim ** (-0.5)
    sums = []
    for cluster in range(rows // per_source):
        at = slice(cluster * per_source, (cluster + 1) * per_source)
        block = jnp.concatenate([got_ref[s, 0, at, :] for s in range(sources)], axis=0)
        query = block[:, :dim]
        keys = block[:, dim : 2 * dim]
        values = block[:, 2 * dim : 3 * dim]
        cotangent = block[:, 3 * dim :]
        live = dot_nt(pick_first, keys) < EMPTY_LEVEL
        allowed = (live & causal) | diagonal
        probs, dscores = softmax_and_grads(query, keys, values, cotangent, None, allowed)
        probs_low = probs.astype(BF16)
        dscores_low = dscores.astype(BF16)
        result = jnp.concatenate(
            [
                dot_nn(probs_low, values).astype(BF16),
                (dot_nn(dscores_low, keys) * scaling).astype(BF16),
                (dot_tn(dscores_low, query) * scaling).astype(BF16),
                dot_tn(probs_low, cotangent).astype(BF16),
            ],
            axis=1,
        )
        for s in range(sources):
            out_ref[s, 0, at, :] = result[s * per_source : (s + 1) * per_source]
        wide = keys.astype(F32)
        sums.append(jnp.sum(jnp.where(first_col & (wide > EMPTY_LEVEL), 0.0, wide), axis=0, keepdims=True))
    key_sums = jnp.concatenate(sums, axis=0)
    norm = jnp.sqrt(jnp.mean(key_sums * key_sums, axis=-1, keepdims=True) + EPSILON)
    centroid_ref[0] = key_sums / norm


def owner(got, per_source):
    sources, heads, rows, width = got.shape
    block = pl.BlockSpec((sources, 1, rows, width), lambda h: (0, h, 0, 0))
    held = rows // per_source
    return pl.pallas_call(
        lambda *refs: owner_kernel(*refs, per_source=per_source),
        grid=(heads,),
        in_specs=[block],
        out_specs=(block, pl.BlockSpec((1, held, HEAD_DIM), lambda h: (h, 0, 0))),
        out_shape=(
            jax.ShapeDtypeStruct(got.shape, BF16),
            jax.ShapeDtypeStruct((heads, held, HEAD_DIM), F32),
        ),
        name="owner",
    )(got)


def unpack_kernel(flat_ref, home_ref, *out_refs):
    tokens = flat_ref.shape[2]
    sources, _, rows, width = home_ref.shape
    lanes = HEAD_DIM
    wide = jnp.broadcast_to(flat_ref[0, :1, :], (lanes, tokens)).T.astype(jnp.int32)
    lane = iota((tokens, lanes), 1)
    slots = sources * rows
    chosen = jnp.concatenate(
        [jnp.where(wide == lane + at, 1.0, 0.0).astype(BF16) for at in range(0, slots, lanes)], axis=1
    )
    moved = dot_nn(chosen, home_ref[:, 0].reshape(slots, width)).astype(BF16)
    for n, out_ref in enumerate(out_refs):
        out_ref[...] = moved[:, n * HEAD_DIM : (n + 1) * HEAD_DIM]


def unpack(flat, home):
    heads, _, tokens = flat.shape
    sources, _, rows, width = home.shape
    outs = width // HEAD_DIM
    column = pl.BlockSpec((tokens, HEAD_DIM), lambda h: (0, h))
    return pl.pallas_call(
        unpack_kernel,
        grid=(heads,),
        in_specs=[
            pl.BlockSpec((1, 8, tokens), lambda h: (h, 0, 0)),
            pl.BlockSpec((sources, 1, rows, width), lambda h: (0, h, 0, 0)),
        ],
        out_specs=(column,) * outs,
        out_shape=(jax.ShapeDtypeStruct((tokens, heads * HEAD_DIM), BF16),) * outs,
        name="unpack",
    )(flat, home)


def shift_rows(array, sign):
    count, lanes = array.shape
    row = iota((count, lanes), 0)
    step = 1
    while step < count:
        rolled = pltpu.roll(array, step if sign > 0 else lanes - step, 1)
        array = jnp.where((row // step) % 2 == 1, rolled, array)
        step *= 2
    return array


def local_kernel(
    first_ref,
    bias_ref,
    q_ref,
    k_ref,
    v_ref,
    g_ref,
    pk_ref,
    pv_ref,
    nq_ref,
    nk_ref,
    nv_ref,
    ng_ref,
    out_ref,
    dq_ref,
    dk_ref,
    dv_ref,
    part_ref,
):
    tokens, dim = q_ref.shape
    scaling = dim ** (-0.5)
    size = (WINDOW, 2 * WINDOW)
    row = iota(size, 0)
    col = iota(size, 1)
    inside = (col > row) & (col <= row + WINDOW)
    inside_first = inside & (col >= WINDOW * first_ref[0, 0])
    bias = shift_rows(jnp.broadcast_to(bias_ref[...], size), 1)
    count = tokens // WINDOW
    total = jnp.zeros(size, F32)
    late_dk = late_dv = None
    for b in range(count + 1):
        at = slice(b * WINDOW, (b + 1) * WINDOW)
        if b < count:
            query, late_k, late_v, cot = q_ref[at], k_ref[at], v_ref[at], g_ref[at]
        else:
            query, late_k, late_v, cot = nq_ref[...], nk_ref[...], nv_ref[...], ng_ref[...]
        behind = slice((b - 1) * WINDOW, b * WINDOW)
        early_k = pk_ref[...] if b == 0 else k_ref[behind]
        early_v = pv_ref[...] if b == 0 else v_ref[behind]
        keys = jnp.concatenate([early_k, late_k], axis=0)
        values = jnp.concatenate([early_v, late_v], axis=0)
        probs, dscores = softmax_and_grads(
            query, keys, values, cot, bias, inside_first if b == 0 else inside
        )
        probs_low = probs.astype(BF16)
        dscores_low = dscores.astype(BF16)
        if b < count:
            total = total + dscores
            out_ref[at] = dot_nn(probs_low, values).astype(BF16)
            dq_ref[at] = (dot_nn(dscores_low, keys) * scaling).astype(BF16)
        if b > 0:
            early_dk = dot_tn(dscores_low[:, :WINDOW], query)
            early_dv = dot_tn(probs_low[:, :WINDOW], cot)
            dk_ref[behind] = ((late_dk + early_dk) * scaling).astype(BF16)
            dv_ref[behind] = (late_dv + early_dv).astype(BF16)
        if b < count:
            late_dk = dot_tn(dscores_low[:, WINDOW:], query)
            late_dv = dot_tn(probs_low[:, WINDOW:], cot)
    part = jnp.sum(shift_rows(total, -1), axis=0, keepdims=True)
    part = jnp.broadcast_to(part, part_ref.shape)

    @pl.when(pl.program_id(0) == 0)
    def _():
        part_ref[...] = part

    @pl.when(pl.program_id(0) > 0)
    def _():
        part_ref[...] += part


def local(first, bias_row, own, behind, ahead, copies):
    tokens, columns = own[0].shape
    heads = columns // HEAD_DIM
    column = pl.BlockSpec((tokens, HEAD_DIM), lambda h: (0, h))

    def halo(n):
        return pl.BlockSpec((WINDOW, HEAD_DIM), lambda h: (0, n * heads + h))

    return pl.pallas_call(
        local_kernel,
        grid=(heads,),
        in_specs=[
            pl.BlockSpec((1, 1), lambda h: (0, 0), memory_space=pltpu.SMEM),
            pl.BlockSpec((1, 2 * WINDOW), lambda h: (0, 0)),
            column,
            column,
            column,
            column,
            halo(0),
            halo(1),
            halo(0),
            halo(1),
            halo(2),
            halo(3),
        ],
        out_specs=(column,) * 4 + (pl.BlockSpec((copies, 2 * WINDOW), lambda h: (0, 0)),),
        out_shape=(jax.ShapeDtypeStruct((tokens, columns), BF16),) * 4
        + (jax.ShapeDtypeStruct((copies, 2 * WINDOW), F32),),
        name="local",
    )(first, bias_row, *own, behind, behind, ahead, ahead, ahead, ahead)


def shards(
    routed_q,
    routed_k,
    routed_v,
    routed_grad,
    local_q,
    local_k,
    local_v,
    local_grad,
    clusters,
    cluster_slot,
    rel_bias,
):
    ctx_size = lax.axis_size("ctx")
    device_count = ctx_size * lax.axis_size("head")
    tokens = routed_q.shape[0]
    per_source = 2 * tokens // cluster_slot.shape[1]

    sent, flat = pack(
        clusters, cluster_slot, (routed_q, routed_k, routed_v, routed_grad), ctx_size, per_source
    )
    got = lax.all_to_all(sent, "ctx", 0, 0, tiled=True)

    tail = jnp.concatenate([local_k[-WINDOW:], local_v[-WINDOW:]], axis=1)
    lead = jnp.concatenate([a[:WINDOW] for a in (local_q, local_k, local_v, local_grad)], axis=1)
    behind = lax.ppermute(tail, "ctx", [(i, i + 1) for i in range(ctx_size - 1)])
    ahead = lax.ppermute(lead, "ctx", [(i + 1, i) for i in range(ctx_size - 1)])
    first = (lax.axis_index("ctx") == 0).astype(jnp.int32).reshape(1, 1)
    bias_row = jnp.concatenate(
        [jnp.zeros((1,), F32), rel_bias[::-1], jnp.zeros((WINDOW - 1,), F32)]
    ).reshape(1, 2 * WINDOW)
    local_out, local_dq, local_dk, local_dv, part = local(
        first, bias_row, (local_q, local_k, local_v, local_grad), behind, ahead, device_count
    )
    parts = lax.all_to_all(part, ("ctx", "head"), 0, 0, tiled=True)
    bias_grad = jnp.sum(parts, axis=0)[1 : WINDOW + 1][::-1]

    back, centroids = owner(got, per_source)
    home = lax.all_to_all(back, "ctx", 0, 0, tiled=True)
    routed_out, routed_dq, routed_dk, routed_dv = unpack(flat, home)
    return (
        routed_out,
        routed_dq,
        routed_dk,
        routed_dv,
        centroids,
        local_out,
        local_dq,
        local_dk,
        local_dv,
        bias_grad,
    )


def solution(mesh):
    return jax.shard_map(
        shards,
        mesh=mesh,
        in_specs=(
            P("ctx", "head"),
            P("ctx", "head"),
            P("ctx", "head"),
            P("ctx", "head"),
            P("ctx", "head"),
            P("ctx", "head"),
            P("ctx", "head"),
            P("ctx", "head"),
            P("head", "ctx"),
            P("head", None),
            P(),
        ),
        out_specs=(
            P("ctx", "head"),
            P("ctx", "head"),
            P("ctx", "head"),
            P("ctx", "head"),
            P("head", "ctx", None),
            P("ctx", "head"),
            P("ctx", "head"),
            P("ctx", "head"),
            P("ctx", "head"),
            P(),
        ),
        check_vma=False,
    )
```

```python
import jax
import jax.numpy as jnp
from jax import lax
from jax.experimental import pallas as pl
from jax.experimental.pallas import tpu as pltpu
from jax.sharding import PartitionSpec as P

HEAD_DIM = 128
WINDOW = 128

NEG = -1e30
EPSILON = 1e-06
EMPTY = 64.0
EMPTY_LEVEL = 32.0

F32 = jnp.float32
BF16 = jnp.bfloat16


def dot_nn(a, b):
    return lax.dot_general(a, b, (((1,), (0,)), ((), ())), preferred_element_type=F32)


def dot_nt(a, b):
    return lax.dot_general(a, b, (((1,), (1,)), ((), ())), preferred_element_type=F32)


def dot_tn(a, b):
    return lax.dot_general(a, b, (((0,), (0,)), ((), ())), preferred_element_type=F32)


def iota(shape, dim):
    return lax.broadcasted_iota(jnp.int32, shape, dim)


def softmax_down(scores, dprobs):
    exponent = jnp.exp(scores - jnp.max(scores, axis=0, keepdims=True))
    probs = exponent * (1.0 / jnp.sum(exponent, axis=0, keepdims=True))
    weighted = probs * dprobs
    return probs, weighted - probs * jnp.sum(weighted, axis=0, keepdims=True)


def pack_kernel(me_ref, ids_ref, slots_ref, q_ref, k_ref, v_ref, g_ref, flat_ref, *out_refs, head, per_source):
    ids = ids_ref[head : head + 1, :]
    tokens = ids.shape[1]
    clusters = slots_ref.shape[1]
    rows = out_refs[0].shape[0]
    member = iota((clusters, tokens), 0) == ids
    member_low = jnp.where(member, 1.0, 0.0).astype(BF16)
    earlier = jnp.where(iota((tokens, tokens), 0) < iota((tokens, tokens), 1), 1.0, 0.0).astype(BF16)
    before = dot_nn(member_low, earlier)
    rank = jnp.sum(jnp.where(member, before, 0.0), axis=0, keepdims=True)
    slots = jnp.broadcast_to(slots_ref[head : head + 1, :], (8, clusters)).astype(F32).astype(BF16)
    flat = dot_nn(slots, member_low)[:1] * per_source + rank
    flat_ref[...] = jnp.broadcast_to(flat, flat_ref.shape)
    where_to = flat.astype(jnp.int32)
    data = jnp.concatenate([q_ref[...], k_ref[...], v_ref[...], g_ref[...]], axis=1)
    dim = k_ref.shape[1]
    me = me_ref[0, 0]
    slot = iota((rows, tokens), 0)
    chosen = [jnp.where(slot == where_to - (me ^ m) * rows, 1.0, 0.0) for m in range(len(out_refs))]
    moved = dot_nn(jnp.concatenate([c.astype(BF16) for c in chosen], axis=0), data)
    first_col = iota((rows, dim), 1) == 0
    for m, out_ref in enumerate(out_refs):
        part = moved[m * rows : (m + 1) * rows]
        filled = jnp.sum(chosen[m], axis=1, keepdims=True) > 0.5
        marked = jnp.where(first_col & ~filled, EMPTY, part[:, dim : 2 * dim])
        out_ref[:, :dim] = part[:, :dim].astype(BF16)
        out_ref[:, dim : 2 * dim] = marked.astype(BF16)
        out_ref[:, 2 * dim :] = part[:, 2 * dim :].astype(BF16)


def scalar_spec():
    return pl.BlockSpec((1, 1), lambda *_: (0, 0), memory_space=pltpu.SMEM)


def whole(array):
    return pl.BlockSpec(array.shape, lambda *_: (0,) * array.ndim)


def pack(me, ids, slots, arrays, head, dests, per_source):
    tokens = arrays[0].shape[0]
    clusters = slots.shape[1]
    rows = clusters * per_source // dests
    width = len(arrays) * HEAD_DIM
    column = pl.BlockSpec((tokens, HEAD_DIM), lambda i: (0, head))
    shapes = [jax.ShapeDtypeStruct((8, tokens), F32)]
    shapes += [jax.ShapeDtypeStruct((rows, width), BF16)] * dests
    flat, *chunks = pl.pallas_call(
        lambda *refs: pack_kernel(*refs, head=head, per_source=per_source),
        grid=(1,),
        in_specs=[scalar_spec(), whole(ids), whole(slots)] + [column] * 4,
        out_specs=[whole(s) for s in shapes],
        out_shape=shapes,
        name="pack",
    )(me, ids, slots, *arrays)
    return flat, chunks


def owner_kernel(me_ref, *refs, per_source, sources):
    got_refs = refs[:sources]
    out_refs = refs[-sources - 1 : -1]
    centroid_ref = refs[-1]
    dim = HEAD_DIM
    capacity = sources * per_source
    clusters = got_refs[0].shape[0] // per_source
    key = iota((capacity, capacity), 0)
    query = iota((capacity, capacity), 1)
    base = me_ref[0, 0] * per_source
    causal = (key ^ base) <= (query ^ base)
    diagonal = key == query
    first_col = iota((capacity, dim), 1) == 0
    scaling = dim ** (-0.5)
    spots = [slice(c * per_source, (c + 1) * per_source) for c in range(clusters)]

    def gathered(part):
        at = slice(part * dim, (part + 1) * dim)
        return [jnp.concatenate([ref[spot, at] for ref in got_refs], axis=0) for spot in spots]

    def scatter(part, results):
        at = slice(part * dim, (part + 1) * dim)
        for spot, result in zip(spots, results):
            for m, ref in enumerate(out_refs):
                ref[spot, at] = result[m * per_source : (m + 1) * per_source].astype(BF16)

    queries, keys, values, cots = (gathered(part) for part in range(4))
    scores, sums = [], []
    for q, k in zip(queries, keys):
        wide = k.astype(F32)
        live = wide[:, :1] < EMPTY_LEVEL
        scores.append(jnp.where((live & causal) | diagonal, dot_nt(k, q) * scaling, NEG))
        sums.append(jnp.sum(jnp.where(first_col & ~live, 0.0, wide), axis=0, keepdims=True))
    dprobs = [dot_nt(v, g) for v, g in zip(values, cots)]
    both = [softmax_down(s, d) for s, d in zip(scores, dprobs)]
    probs = [p.astype(BF16) for p, _ in both]
    dscores = [d.astype(BF16) for _, d in both]
    scatter(0, [dot_tn(p, v) for p, v in zip(probs, values)])
    scatter(3, [dot_nn(p, g) for p, g in zip(probs, cots)])
    scatter(2, [dot_nn(d, q) * scaling for d, q in zip(dscores, queries)])
    scatter(1, [dot_tn(d, k) * scaling for d, k in zip(dscores, keys)])
    key_sums = jnp.concatenate(sums, axis=0)
    norm = jnp.sqrt(jnp.mean(key_sums * key_sums, axis=-1, keepdims=True) + EPSILON)
    centroid_ref[0] = key_sums / norm


def owner(me, got, per_source, head, heads, previous):
    rows, width = got[0].shape
    shapes = [jax.ShapeDtypeStruct((rows, width), BF16)] * len(got)
    held = jax.ShapeDtypeStruct((heads, rows // per_source, HEAD_DIM), F32)
    any_spec = pl.BlockSpec(memory_space=pl.ANY)
    *back, centroids = pl.pallas_call(
        lambda *refs: owner_kernel(*refs, per_source=per_source, sources=len(got)),
        grid=(1,),
        in_specs=[scalar_spec()] + [whole(g) for g in got] + [any_spec] * len(previous),
        out_specs=[whole(s) for s in shapes]
        + [pl.BlockSpec((1,) + held.shape[1:], lambda i: (head, 0, 0))],
        out_shape=shapes + [held],
        input_output_aliases={1 + len(got) + n: len(got) + n for n in range(len(previous))},
        name="owner",
    )(me, *got, *previous)
    return back, centroids


def unpack_kernel(me_ref, flat_ref, *refs, chunks):
    home_refs = refs[:chunks]
    width = home_refs[0].shape[1]
    out_refs = refs[-(width // HEAD_DIM) :]
    tokens = flat_ref.shape[1]
    rows = home_refs[0].shape[0]
    wide = jnp.broadcast_to(flat_ref[:1, :], (HEAD_DIM, tokens)).T.astype(jnp.int32)[:, :rows]
    lane = iota((tokens, rows), 1)
    chosen = jnp.concatenate(
        [
            jnp.where(wide - (me_ref[0, 0] ^ m) * rows == lane, 1.0, 0.0).astype(BF16)
            for m in range(chunks)
        ],
        axis=1,
    )
    home = jnp.concatenate([ref[...] for ref in home_refs], axis=0)
    moved = dot_nn(chosen, home).astype(BF16)
    for n, out_ref in enumerate(out_refs):
        out_ref[...] = moved[:, n * HEAD_DIM : (n + 1) * HEAD_DIM]


def unpack(me, flat, home, head, heads, previous):
    tokens = flat.shape[1]
    outs = home[0].shape[1] // HEAD_DIM
    any_spec = pl.BlockSpec(memory_space=pl.ANY)
    return pl.pallas_call(
        lambda *refs: unpack_kernel(*refs, chunks=len(home)),
        grid=(1,),
        in_specs=[scalar_spec(), whole(flat)] + [whole(h) for h in home] + [any_spec] * len(previous),
        out_specs=[pl.BlockSpec((tokens, HEAD_DIM), lambda i: (0, head))] * outs,
        out_shape=[jax.ShapeDtypeStruct((tokens, heads * HEAD_DIM), BF16)] * outs,
        input_output_aliases={2 + len(home) + n: n for n in range(len(previous))},
        name="unpack",
    )(me, flat, *home, *previous)


def exchange(chunks):
    size = len(chunks)
    moved = [chunks[0]] + [None] * (size - 1)
    for m in reversed(range(1, size)):
        moved[m] = lax.ppermute(chunks[m], "ctx", [(i, i ^ m) for i in range(size)])
    return moved


def shift_rows(array, sign):
    count, lanes = array.shape
    row = iota((count, lanes), 0)
    step = 1
    while step < count:
        rolled = pltpu.roll(array, step if sign > 0 else lanes - step, 1)
        array = jnp.where((row & step) != 0, rolled, array)
        step *= 2
    return array


def local_kernel(
    first_ref,
    bias_ref,
    q_ref,
    k_ref,
    v_ref,
    g_ref,
    pk_ref,
    pv_ref,
    nq_ref,
    nk_ref,
    nv_ref,
    ng_ref,
    out_ref,
    dq_ref,
    dk_ref,
    dv_ref,
    part_ref,
):
    tokens, dim = q_ref.shape
    scaling = dim ** (-0.5)
    count = tokens // WINDOW
    size = (WINDOW, WINDOW)
    early = iota(size, 1) < iota(size, 0)
    bias = shift_rows(jnp.broadcast_to(bias_ref[...], size), 1)
    bias_first = jnp.where(early & (first_ref[0, 0] > 0), NEG, bias)
    spots = [slice(b * WINDOW, (b + 1) * WINDOW) for b in range(count)]
    queries = [q_ref[s] for s in spots] + [nq_ref[...]]
    cots = [g_ref[s] for s in spots] + [ng_ref[...]]
    keys = [pk_ref[...]] + [k_ref[s] for s in spots] + [nk_ref[...]]
    values = [pv_ref[...]] + [v_ref[s] for s in spots] + [nv_ref[...]]
    scores = [
        jnp.where(early, dot_nt(keys[b], queries[b]), dot_nt(keys[b + 1], queries[b])) * scaling
        + (bias if b else bias_first)
        for b in range(count + 1)
    ]
    dprobs = [
        jnp.where(early, dot_nt(values[b], cots[b]), dot_nt(values[b + 1], cots[b]))
        for b in range(count + 1)
    ]
    both = [softmax_down(s, d) for s, d in zip(scores, dprobs)]
    total = both[0][1]
    for b in range(1, count):
        total = total + both[b][1]
    zero = jnp.zeros(size, F32)
    probs = [
        (jnp.where(early, p, zero).astype(BF16), jnp.where(early, zero, p).astype(BF16)) for p, _ in both
    ]
    dscores = [
        (jnp.where(early, d, zero).astype(BF16), jnp.where(early, zero, d).astype(BF16)) for _, d in both
    ]
    for b, s in enumerate(spots):
        out_ref[s] = (dot_tn(probs[b][0], values[b]) + dot_tn(probs[b][1], values[b + 1])).astype(BF16)
        dv_ref[s] = (dot_nn(probs[b][1], cots[b]) + dot_nn(probs[b + 1][0], cots[b + 1])).astype(BF16)
        dk = dot_nn(dscores[b][1], queries[b]) + dot_nn(dscores[b + 1][0], queries[b + 1])
        dk_ref[s] = (dk * scaling).astype(BF16)
        dq = dot_tn(dscores[b][0], keys[b]) + dot_tn(dscores[b][1], keys[b + 1])
        dq_ref[s] = (dq * scaling).astype(BF16)
    part = jnp.sum(shift_rows(total, -1), axis=0, keepdims=True)
    part = jnp.broadcast_to(part[None], part_ref.shape)

    @pl.when(pl.program_id(0) == 0)
    def _():
        part_ref[...] = part

    @pl.when(pl.program_id(0) > 0)
    def _():
        part_ref[...] += part


def local(first, rel_bias, own, behind, ahead, copies):
    tokens, columns = own[0].shape
    heads = columns // HEAD_DIM
    column = pl.BlockSpec((tokens, HEAD_DIM), lambda h: (0, h))

    def halo(n):
        return pl.BlockSpec((WINDOW, HEAD_DIM), lambda h: (0, n * heads + h))

    part = jax.ShapeDtypeStruct((copies, 8, WINDOW), F32)
    return pl.pallas_call(
        local_kernel,
        grid=(heads,),
        in_specs=[scalar_spec(), whole(rel_bias)]
        + [column] * 4
        + [halo(0), halo(1), halo(0), halo(1), halo(2), halo(3)],
        out_specs=[column] * 4 + [whole(part)],
        out_shape=[jax.ShapeDtypeStruct((tokens, columns), BF16)] * 4 + [part],
        name="local",
    )(first, rel_bias, *own, behind, behind, ahead, ahead, ahead, ahead)


def shards(
    routed_q,
    routed_k,
    routed_v,
    routed_grad,
    local_q,
    local_k,
    local_v,
    local_grad,
    clusters,
    cluster_slot,
    rel_bias,
):
    ctx_size = lax.axis_size("ctx")
    device_count = ctx_size * lax.axis_size("head")
    tokens = routed_q.shape[0]
    per_source = 2 * tokens // cluster_slot.shape[1]

    heads = cluster_slot.shape[0]
    me = lax.axis_index("ctx").reshape(1, 1)
    routed = (routed_q, routed_k, routed_v, routed_grad)
    flats, got = [], []
    for head in range(heads):
        flat, chunks = pack(me, clusters, cluster_slot, routed, head, ctx_size, per_source)
        flats.append(flat)
        got.append(exchange(chunks))

    tail = jnp.concatenate([local_k[-WINDOW:], local_v[-WINDOW:]], axis=1)
    lead = jnp.concatenate([a[:WINDOW] for a in (local_q, local_k, local_v, local_grad)], axis=1)
    behind = lax.ppermute(tail, "ctx", [(i, i + 1) for i in range(ctx_size - 1)])
    ahead = lax.ppermute(lead, "ctx", [(i + 1, i) for i in range(ctx_size - 1)])
    first = (lax.axis_index("ctx") == 0).astype(jnp.int32).reshape(1, 1)
    local_out, local_dq, local_dk, local_dv, part = local(
        first, rel_bias.reshape(1, WINDOW), (local_q, local_k, local_v, local_grad), behind, ahead, device_count
    )
    parts = lax.all_to_all(part, ("ctx", "head"), 0, 0, tiled=True)
    bias_grad = jnp.sum(parts[:, 0], axis=0)

    centroids, columns = (), ()
    for head in range(heads):
        back, *centroids = owner(me, got[head], per_source, head, heads, centroids)
        columns = unpack(me, flats[head], exchange(back), head, heads, columns)
    routed_out, routed_dq, routed_dk, routed_dv = columns
    (centroids,) = centroids
    return (
        routed_out,
        routed_dq,
        routed_dk,
        routed_dv,
        centroids,
        local_out,
        local_dq,
        local_dk,
        local_dv,
        bias_grad,
    )


def solution(mesh):
    return jax.shard_map(
        shards,
        mesh=mesh,
        in_specs=(
            P("ctx", "head"),
            P("ctx", "head"),
            P("ctx", "head"),
            P("ctx", "head"),
            P("ctx", "head"),
            P("ctx", "head"),
            P("ctx", "head"),
            P("ctx", "head"),
            P("head", "ctx"),
            P("head", None),
            P(),
        ),
        out_specs=(
            P("ctx", "head"),
            P("ctx", "head"),
            P("ctx", "head"),
            P("ctx", "head"),
            P("head", "ctx", None),
            P("ctx", "head"),
            P("ctx", "head"),
            P("ctx", "head"),
            P("ctx", "head"),
            P(),
        ),
        check_vma=False,
    )
```

```python
import jax
import jax.numpy as jnp
from jax import lax
from jax.experimental import pallas as pl
from jax.experimental.pallas import tpu as pltpu
from jax.sharding import PartitionSpec as P


HEAD_DIM = 128
WINDOW = 128

NEG = -1e30
EPSILON = 1e-06
EMPTY = 64.0
EMPTY_LEVEL = 32.0

PARAMS = pltpu.CompilerParams(vmem_limit_bytes=16 << 20)

F32 = jnp.float32
BF16 = jnp.bfloat16


def dot_nn(a, b):
    return lax.dot_general(a, b, (((1,), (0,)), ((), ())), preferred_element_type=F32)


def dot_nt(a, b):
    return lax.dot_general(a, b, (((1,), (1,)), ((), ())), preferred_element_type=F32)


def dot_tn(a, b):
    return lax.dot_general(a, b, (((0,), (0,)), ((), ())), preferred_element_type=F32)


def iota(shape, dim):
    return lax.broadcasted_iota(jnp.int32, shape, dim)


def softmax_down(scores, dprobs):
    exponent = jnp.exp(scores - jnp.max(scores, axis=0, keepdims=True))
    probs = exponent * (1.0 / jnp.sum(exponent, axis=0, keepdims=True))
    weighted = probs * dprobs
    return probs, weighted - probs * jnp.sum(weighted, axis=0, keepdims=True)


def pack_kernel(me_ref, ids_ref, slots_ref, q_ref, k_ref, v_ref, g_ref, flat_ref, *out_refs, head, per_source):
    ids = ids_ref[head : head + 1, :]
    tokens = ids.shape[1]
    clusters = slots_ref.shape[1]
    rows = out_refs[0].shape[0]
    member = iota((clusters, tokens), 0) == ids
    member_low = jnp.where(member, 1.0, 0.0).astype(BF16)
    earlier = jnp.where(iota((tokens, tokens), 0) < iota((tokens, tokens), 1), 1.0, 0.0).astype(BF16)
    before = dot_nn(member_low, earlier)
    rank = jnp.sum(jnp.where(member, before, 0.0), axis=0, keepdims=True)
    slots = jnp.broadcast_to(slots_ref[head : head + 1, :], (8, clusters)).astype(F32).astype(BF16)
    flat = dot_nn(slots, member_low)[:1] * per_source + rank
    flat_ref[...] = jnp.broadcast_to(flat, flat_ref.shape)
    where_to = flat.astype(jnp.int32)
    data = jnp.concatenate([q_ref[...], k_ref[...], v_ref[...], g_ref[...]], axis=1)
    dim = k_ref.shape[1]
    me = me_ref[0, 0]
    slot = iota((rows, tokens), 0)
    chosen = [jnp.where(slot == where_to - (me ^ m) * rows, 1.0, 0.0) for m in range(len(out_refs))]
    moved = dot_nn(jnp.concatenate([c.astype(BF16) for c in chosen], axis=0), data)
    first_col = iota((rows, dim), 1) == 0
    for m, out_ref in enumerate(out_refs):
        part = moved[m * rows : (m + 1) * rows]
        filled = jnp.sum(chosen[m], axis=1, keepdims=True) > 0.5
        marked = jnp.where(first_col & ~filled, EMPTY, part[:, dim : 2 * dim])
        out_ref[:, :dim] = part[:, :dim].astype(BF16)
        out_ref[:, dim : 2 * dim] = marked.astype(BF16)
        out_ref[:, 2 * dim :] = part[:, 2 * dim :].astype(BF16)


def scalar_spec():
    return pl.BlockSpec((1, 1), lambda *_: (0, 0), memory_space=pltpu.SMEM)


def whole(array):
    return pl.BlockSpec(array.shape, lambda *_: (0,) * array.ndim)


def pack(me, ids, slots, arrays, head, dests, per_source):
    tokens = arrays[0].shape[0]
    clusters = slots.shape[1]
    rows = clusters * per_source // dests
    width = len(arrays) * HEAD_DIM
    column = pl.BlockSpec((tokens, HEAD_DIM), lambda i: (0, head))
    shapes = [jax.ShapeDtypeStruct((8, tokens), F32)]
    shapes += [jax.ShapeDtypeStruct((rows, width), BF16)] * dests
    flat, *chunks = pl.pallas_call(
        lambda *refs: pack_kernel(*refs, head=head, per_source=per_source),
        grid=(1,),
        in_specs=[scalar_spec(), whole(ids), whole(slots)] + [column] * 4,
        out_specs=[whole(s) for s in shapes],
        out_shape=shapes,
        name="pack",
        compiler_params=PARAMS,
    )(me, ids, slots, *arrays)
    return flat, chunks


def owner_kernel(me_ref, *refs, per_source, sources):
    got_refs = refs[:sources]
    out_refs = refs[-sources - 1 : -1]
    centroid_ref = refs[-1]
    dim = HEAD_DIM
    capacity = sources * per_source
    clusters = got_refs[0].shape[0] // per_source
    key = iota((capacity, capacity), 0)
    query = iota((capacity, capacity), 1)
    base = me_ref[0, 0] * per_source
    causal = (key ^ base) <= (query ^ base)
    diagonal = key == query
    first_col = iota((capacity, dim), 1) == 0
    scaling = dim ** (-0.5)
    spots = [slice(c * per_source, (c + 1) * per_source) for c in range(clusters)]

    def gathered(part):
        at = slice(part * dim, (part + 1) * dim)
        return [jnp.concatenate([ref[spot, at] for ref in got_refs], axis=0) for spot in spots]

    def scatter(part, results):
        at = slice(part * dim, (part + 1) * dim)
        for spot, result in zip(spots, results):
            for m, ref in enumerate(out_refs):
                ref[spot, at] = result[m * per_source : (m + 1) * per_source].astype(BF16)

    queries, keys, values, cots = (gathered(part) for part in range(4))
    scores, sums = [], []
    for q, k in zip(queries, keys):
        wide = k.astype(F32)
        live = wide[:, :1] < EMPTY_LEVEL
        scores.append(jnp.where((live & causal) | diagonal, dot_nt(k, q) * scaling, NEG))
        sums.append(jnp.sum(jnp.where(first_col & ~live, 0.0, wide), axis=0, keepdims=True))
    dprobs = [dot_nt(v, g) for v, g in zip(values, cots)]
    both = [softmax_down(s, d) for s, d in zip(scores, dprobs)]
    probs = [p.astype(BF16) for p, _ in both]
    dscores = [d.astype(BF16) for _, d in both]
    scatter(0, [dot_tn(p, v) for p, v in zip(probs, values)])
    scatter(3, [dot_nn(p, g) for p, g in zip(probs, cots)])
    scatter(2, [dot_nn(d, q) * scaling for d, q in zip(dscores, queries)])
    scatter(1, [dot_tn(d, k) * scaling for d, k in zip(dscores, keys)])
    key_sums = jnp.concatenate(sums, axis=0)
    norm = jnp.sqrt(jnp.mean(key_sums * key_sums, axis=-1, keepdims=True) + EPSILON)
    centroid_ref[0] = key_sums / norm


def owner(me, got, per_source, head, heads, previous):
    rows, width = got[0].shape
    shapes = [jax.ShapeDtypeStruct((rows, width), BF16)] * len(got)
    held = jax.ShapeDtypeStruct((heads, rows // per_source, HEAD_DIM), F32)
    any_spec = pl.BlockSpec(memory_space=pl.ANY)
    *back, centroids = pl.pallas_call(
        lambda *refs: owner_kernel(*refs, per_source=per_source, sources=len(got)),
        grid=(1,),
        in_specs=[scalar_spec()] + [whole(g) for g in got] + [any_spec] * len(previous),
        out_specs=[whole(s) for s in shapes]
        + [pl.BlockSpec((1,) + held.shape[1:], lambda i: (head, 0, 0))],
        out_shape=shapes + [held],
        input_output_aliases={1 + len(got) + n: len(got) + n for n in range(len(previous))},
        name="owner",
        compiler_params=PARAMS,
    )(me, *got, *previous)
    return back, centroids


def unpack_kernel(me_ref, flat_ref, *refs, chunks):
    home_refs = refs[:chunks]
    width = home_refs[0].shape[1]
    out_refs = refs[-(width // HEAD_DIM) :]
    tokens = flat_ref.shape[1]
    rows = home_refs[0].shape[0]
    wide = jnp.broadcast_to(flat_ref[:1, :], (HEAD_DIM, tokens)).T.astype(jnp.int32)[:, :rows]
    lane = iota((tokens, rows), 1)
    chosen = jnp.concatenate(
        [
            jnp.where(wide - (me_ref[0, 0] ^ m) * rows == lane, 1.0, 0.0).astype(BF16)
            for m in range(chunks)
        ],
        axis=1,
    )
    home = jnp.concatenate([ref[...] for ref in home_refs], axis=0)
    moved = dot_nn(chosen, home).astype(BF16)
    for n, out_ref in enumerate(out_refs):
        out_ref[...] = moved[:, n * HEAD_DIM : (n + 1) * HEAD_DIM]


def unpack(me, flat, home, head, heads, previous):
    tokens = flat.shape[1]
    outs = home[0].shape[1] // HEAD_DIM
    any_spec = pl.BlockSpec(memory_space=pl.ANY)
    return pl.pallas_call(
        lambda *refs: unpack_kernel(*refs, chunks=len(home)),
        grid=(1,),
        in_specs=[scalar_spec(), whole(flat)] + [whole(h) for h in home] + [any_spec] * len(previous),
        out_specs=[pl.BlockSpec((tokens, HEAD_DIM), lambda i: (0, head))] * outs,
        out_shape=[jax.ShapeDtypeStruct((tokens, heads * HEAD_DIM), BF16)] * outs,
        input_output_aliases={2 + len(home) + n: n for n in range(len(previous))},
        name="unpack",
        compiler_params=PARAMS,
    )(me, flat, *home, *previous)


def exchange(chunks):
    size = len(chunks)
    moved = [chunks[0]] + [None] * (size - 1)
    for m in reversed(range(1, size)):
        moved[m] = lax.ppermute(chunks[m], "ctx", [(i, i ^ m) for i in range(size)])
    return moved


def shift_rows(array, sign):
    count, lanes = array.shape
    row = iota((count, lanes), 0)
    step = 1
    while step < count:
        rolled = pltpu.roll(array, step if sign > 0 else lanes - step, 1)
        array = jnp.where((row & step) != 0, rolled, array)
        step *= 2
    return array


def halo_kernel(hq_ref, hk_ref, hv_ref, hg_ref, tk_ref, tv_ref, lead_ref, tail_ref):
    width = hq_ref.shape[1]
    for n, ref in enumerate((hq_ref, hk_ref, hv_ref, hg_ref)):
        lead_ref[:, n * width : (n + 1) * width] = ref[...]
    for n, ref in enumerate((tk_ref, tv_ref)):
        tail_ref[:, n * width : (n + 1) * width] = ref[...]


def halo_pieces(own):
    tokens, width = own[0].shape
    head = pl.BlockSpec((WINDOW, width), lambda i: (0, 0))
    last = pl.BlockSpec((WINDOW, width), lambda i: (tokens // WINDOW - 1, 0))
    shapes = [jax.ShapeDtypeStruct((WINDOW, n * width), BF16) for n in (4, 2)]
    return pl.pallas_call(
        halo_kernel,
        grid=(1,),
        in_specs=[head] * 4 + [last] * 2,
        out_specs=[whole(s) for s in shapes],
        out_shape=shapes,
        name="halo",
        compiler_params=PARAMS,
    )(*own, own[1], own[2])


def local_kernel(
    first_ref,
    bias_ref,
    q_ref,
    k_ref,
    v_ref,
    g_ref,
    pk_ref,
    pv_ref,
    nq_ref,
    nk_ref,
    nv_ref,
    ng_ref,
    out_ref,
    dq_ref,
    dk_ref,
    dv_ref,
    part_ref,
):
    tokens, dim = q_ref.shape
    scaling = dim ** (-0.5)
    count = tokens // WINDOW
    size = (WINDOW, WINDOW)
    early = iota(size, 1) < iota(size, 0)
    bias = shift_rows(jnp.broadcast_to(bias_ref[...], size), 1)
    bias_first = jnp.where(early & (first_ref[0, 0] > 0), NEG, bias)
    spots = [slice(b * WINDOW, (b + 1) * WINDOW) for b in range(count)]
    queries = [q_ref[s] for s in spots] + [nq_ref[...]]
    cots = [g_ref[s] for s in spots] + [ng_ref[...]]
    keys = [pk_ref[...]] + [k_ref[s] for s in spots] + [nk_ref[...]]
    values = [pv_ref[...]] + [v_ref[s] for s in spots] + [nv_ref[...]]
    scores = [
        jnp.where(early, dot_nt(keys[b], queries[b]), dot_nt(keys[b + 1], queries[b])) * scaling
        + (bias if b else bias_first)
        for b in range(count + 1)
    ]
    dprobs = [
        jnp.where(early, dot_nt(values[b], cots[b]), dot_nt(values[b + 1], cots[b]))
        for b in range(count + 1)
    ]
    both = [softmax_down(s, d) for s, d in zip(scores, dprobs)]
    total = both[0][1]
    for b in range(1, count):
        total = total + both[b][1]
    zero = jnp.zeros(size, F32)
    probs = [
        (jnp.where(early, p, zero).astype(BF16), jnp.where(early, zero, p).astype(BF16)) for p, _ in both
    ]
    dscores = [
        (jnp.where(early, d, zero).astype(BF16), jnp.where(early, zero, d).astype(BF16)) for _, d in both
    ]
    for b, s in enumerate(spots):
        out_ref[s] = (dot_tn(probs[b][0], values[b]) + dot_tn(probs[b][1], values[b + 1])).astype(BF16)
        dv_ref[s] = (dot_nn(probs[b][1], cots[b]) + dot_nn(probs[b + 1][0], cots[b + 1])).astype(BF16)
        dk = dot_nn(dscores[b][1], queries[b]) + dot_nn(dscores[b + 1][0], queries[b + 1])
        dk_ref[s] = (dk * scaling).astype(BF16)
        dq = dot_tn(dscores[b][0], keys[b]) + dot_tn(dscores[b][1], keys[b + 1])
        dq_ref[s] = (dq * scaling).astype(BF16)
    part = jnp.sum(shift_rows(total, -1), axis=0, keepdims=True)
    part = jnp.broadcast_to(part[None], part_ref.shape)

    @pl.when(pl.program_id(0) == 0)
    def _():
        part_ref[...] = part

    @pl.when(pl.program_id(0) > 0)
    def _():
        part_ref[...] += part


def local(first, rel_bias, own, behind, ahead, copies):
    tokens, columns = own[0].shape
    heads = columns // HEAD_DIM
    column = pl.BlockSpec((tokens, HEAD_DIM), lambda h: (0, h))

    def halo(n):
        return pl.BlockSpec((WINDOW, HEAD_DIM), lambda h: (0, n * heads + h))

    part = jax.ShapeDtypeStruct((copies, 8, WINDOW), F32)
    return pl.pallas_call(
        local_kernel,
        grid=(heads,),
        in_specs=[scalar_spec(), whole(rel_bias)]
        + [column] * 4
        + [halo(0), halo(1), halo(0), halo(1), halo(2), halo(3)],
        out_specs=[column] * 4 + [whole(part)],
        out_shape=[jax.ShapeDtypeStruct((tokens, columns), BF16)] * 4 + [part],
        name="local",
        compiler_params=PARAMS,
    )(first, rel_bias, *own, behind, behind, ahead, ahead, ahead, ahead)


def shards(
    routed_q,
    routed_k,
    routed_v,
    routed_grad,
    local_q,
    local_k,
    local_v,
    local_grad,
    clusters,
    cluster_slot,
    rel_bias,
):
    ctx_size = lax.axis_size("ctx")
    device_count = ctx_size * lax.axis_size("head")
    tokens = routed_q.shape[0]
    per_source = 2 * tokens // cluster_slot.shape[1]

    heads = cluster_slot.shape[0]
    me = lax.axis_index("ctx").reshape(1, 1)
    in_hbm = lambda arrays: tuple(pltpu.with_memory_space_constraint(a, pltpu.HBM) for a in arrays)
    routed = in_hbm((routed_q, routed_k, routed_v, routed_grad))
    own = in_hbm((local_q, local_k, local_v, local_grad))

    flats, got = [], []
    for head in range(heads):
        flat, chunks = pack(me, clusters, cluster_slot, routed, head, ctx_size, per_source)
        flats.append(flat)
        got.append(exchange(chunks))

    lead, tail = halo_pieces(own)
    behind = lax.ppermute(tail, "ctx", [(i, i + 1) for i in range(ctx_size - 1)])
    ahead = lax.ppermute(lead, "ctx", [(i + 1, i) for i in range(ctx_size - 1)])

    centroids, home = (), []
    for head in range(heads):
        back, *centroids = owner(me, got[head], per_source, head, heads, centroids)
        home.append(exchange(back))
    (centroids,) = centroids

    first = (lax.axis_index("ctx") == 0).astype(jnp.int32).reshape(1, 1)
    local_out, local_dq, local_dk, local_dv, part = local(
        first, rel_bias.reshape(1, WINDOW), own, behind, ahead, device_count
    )
    parts = lax.all_to_all(part, ("ctx", "head"), 0, 0, tiled=True)
    bias_grad = jnp.sum(parts[:, 0], axis=0)

    columns = ()
    for head in range(heads):
        columns = unpack(me, flats[head], home[head], head, heads, columns)
    routed_out, routed_dq, routed_dk, routed_dv = columns
    return (
        routed_out,
        routed_dq,
        routed_dk,
        routed_dv,
        centroids,
        local_out,
        local_dq,
        local_dk,
        local_dv,
        bias_grad,
    )


def solution(mesh):
    return jax.shard_map(
        shards,
        mesh=mesh,
        in_specs=(
            P("ctx", "head"),
            P("ctx", "head"),
            P("ctx", "head"),
            P("ctx", "head"),
            P("ctx", "head"),
            P("ctx", "head"),
            P("ctx", "head"),
            P("ctx", "head"),
            P("head", "ctx"),
            P("head", None),
            P(),
        ),
        out_specs=(
            P("ctx", "head"),
            P("ctx", "head"),
            P("ctx", "head"),
            P("ctx", "head"),
            P("head", "ctx", None),
            P("ctx", "head"),
            P("ctx", "head"),
            P("ctx", "head"),
            P("ctx", "head"),
            P(),
        ),
        check_vma=False,
    )
```

```python
import jax
import jax.numpy as jnp
from jax import lax
from jax.experimental import pallas as pl
from jax.experimental.pallas import tpu as pltpu
from jax.sharding import PartitionSpec as P


HEAD_DIM = 128
WINDOW = 128

NEG = -1e30
EPSILON = 1e-06
EMPTY = 64.0
EMPTY_LEVEL = 32.0

PARAMS = pltpu.CompilerParams(vmem_limit_bytes=16 << 20)

F32 = jnp.float32
BF16 = jnp.bfloat16


def dot_nn(a, b):
    return lax.dot_general(a, b, (((1,), (0,)), ((), ())), preferred_element_type=F32)


def dot_nt(a, b):
    return lax.dot_general(a, b, (((1,), (1,)), ((), ())), preferred_element_type=F32)


def dot_tn(a, b):
    return lax.dot_general(a, b, (((0,), (0,)), ((), ())), preferred_element_type=F32)


def iota(shape, dim):
    return lax.broadcasted_iota(jnp.int32, shape, dim)


def softmax_down(scores, dprobs):
    exponent = jnp.exp(scores - jnp.max(scores, axis=0, keepdims=True))
    probs = exponent * (1.0 / jnp.sum(exponent, axis=0, keepdims=True))
    weighted = probs * dprobs
    return probs, weighted - probs * jnp.sum(weighted, axis=0, keepdims=True)


def pack_kernel(me_ref, ids_ref, slots_ref, q_ref, k_ref, v_ref, g_ref, *refs, head, per_source, halo):
    halo_refs, (flat_ref, *out_refs) = refs[:halo], refs[halo:]
    if halo:
        *out_refs, lead_ref, tail_ref = out_refs
        split = (lead_ref, halo_refs[:4]), (tail_ref, halo_refs[4:])
        for to_ref, from_refs in split:
            for n, ref in enumerate(from_refs):
                to_ref[:, n * ref.shape[1] : (n + 1) * ref.shape[1]] = ref[...]
    ids = ids_ref[head : head + 1, :]
    tokens = ids.shape[1]
    clusters = slots_ref.shape[1]
    rows = out_refs[0].shape[0] // 2
    member = iota((clusters, tokens), 0) == ids
    member_low = jnp.where(member, 1.0, 0.0).astype(BF16)
    earlier = jnp.where(iota((tokens, tokens), 0) < iota((tokens, tokens), 1), 1.0, 0.0).astype(BF16)
    before = dot_nn(member_low, earlier)
    rank = jnp.sum(jnp.where(member, before, 0.0), axis=0, keepdims=True)
    slots = jnp.broadcast_to(slots_ref[head : head + 1, :], (8, clusters)).astype(F32).astype(BF16)
    flat = dot_nn(slots, member_low)[:1] * per_source + rank
    flat_ref[...] = jnp.broadcast_to(flat, flat_ref.shape)
    where_to = flat.astype(jnp.int32)
    data = jnp.concatenate([q_ref[...], k_ref[...], v_ref[...], g_ref[...]], axis=1)
    dim = k_ref.shape[1]
    me = me_ref[0, 0]
    slot = iota((rows, tokens), 0)
    chosen = [jnp.where(slot == where_to - (me ^ m) * rows, 1.0, 0.0) for m in range(2 * len(out_refs))]
    moved = dot_nn(jnp.concatenate([c.astype(BF16) for c in chosen], axis=0), data)
    first_col = iota((rows, dim), 1) == 0
    for m in range(2 * len(out_refs)):
        out_ref = out_refs[m // 2]
        at = slice(m % 2 * rows, (m % 2 + 1) * rows)
        part = moved[m * rows : (m + 1) * rows]
        filled = jnp.sum(chosen[m], axis=1, keepdims=True) > 0.5
        marked = jnp.where(first_col & ~filled, EMPTY, part[:, dim : 2 * dim])
        out_ref[at, :dim] = part[:, :dim].astype(BF16)
        out_ref[at, dim : 2 * dim] = marked.astype(BF16)
        out_ref[at, 2 * dim :] = part[:, 2 * dim :].astype(BF16)


def scalar_spec():
    return pl.BlockSpec((1, 1), lambda *_: (0, 0), memory_space=pltpu.SMEM)


def whole(array):
    return pl.BlockSpec(array.shape, lambda *_: (0,) * array.ndim)


def pack(me, ids, slots, arrays, head, dests, per_source, own):
    tokens = arrays[0].shape[0]
    clusters = slots.shape[1]
    rows = clusters * per_source // dests
    width = len(arrays) * HEAD_DIM
    column = pl.BlockSpec((tokens, HEAD_DIM), lambda i: (0, head))
    shapes = [jax.ShapeDtypeStruct((8, tokens), F32)]
    shapes += [jax.ShapeDtypeStruct((2 * rows, width), BF16)] * (dests // 2)
    operands, specs = [], []
    if own:
        columns = own[0].shape[1]
        first = pl.BlockSpec((WINDOW, columns), lambda i: (0, 0))
        last = pl.BlockSpec((WINDOW, columns), lambda i: (tokens // WINDOW - 1, 0))
        operands = [*own, own[1], own[2]]
        specs = [first] * 4 + [last] * 2
        shapes += [jax.ShapeDtypeStruct((WINDOW, n * columns), BF16) for n in (4, 2)]
    flat, *chunks = pl.pallas_call(
        lambda *refs: pack_kernel(*refs, head=head, per_source=per_source, halo=len(operands)),
        grid=(1,),
        in_specs=[scalar_spec(), whole(ids), whole(slots)] + [column] * 4 + specs,
        out_specs=[whole(s) for s in shapes],
        out_shape=shapes,
        name="pack",
        compiler_params=PARAMS,
    )(me, ids, slots, *arrays, *operands)
    return flat, chunks


def owner_kernel(me_ref, *refs, per_source, sources):
    got_refs = refs[:sources]
    out_refs = refs[-sources // 2 - 1 : -1]
    centroid_ref = refs[-1]
    dim = HEAD_DIM
    capacity = sources * per_source
    rows = got_refs[0].shape[0] // 2
    clusters = rows // per_source
    key = iota((capacity, capacity), 0)
    query = iota((capacity, capacity), 1)
    base = me_ref[0, 0] * per_source
    causal = (key ^ base) <= (query ^ base)
    diagonal = key == query
    first_col = iota((capacity, dim), 1) == 0
    scaling = dim ** (-0.5)
    spots = [c * per_source for c in range(clusters)]

    def gathered(part):
        at = slice(part * dim, (part + 1) * dim)
        return [
            jnp.concatenate(
                [ref[m % 2 * rows + spot : m % 2 * rows + spot + per_source, at] for m, ref in enumerate(got_refs)],
                axis=0,
            )
            for spot in spots
        ]

    def scatter(part, results):
        at = slice(part * dim, (part + 1) * dim)
        for spot, result in zip(spots, results):
            for m in range(sources):
                to = m % 2 * rows + spot
                out_refs[m // 2][to : to + per_source, at] = result[
                    m * per_source : (m + 1) * per_source
                ].astype(BF16)

    queries, keys, values, cots = (gathered(part) for part in range(4))
    scores, sums = [], []
    for q, k in zip(queries, keys):
        wide = k.astype(F32)
        live = wide[:, :1] < EMPTY_LEVEL
        scores.append(jnp.where((live & causal) | diagonal, dot_nt(k, q) * scaling, NEG))
        sums.append(jnp.sum(jnp.where(first_col & ~live, 0.0, wide), axis=0, keepdims=True))
    dprobs = [dot_nt(v, g) for v, g in zip(values, cots)]
    both = [softmax_down(s, d) for s, d in zip(scores, dprobs)]
    probs = [p.astype(BF16) for p, _ in both]
    dscores = [d.astype(BF16) for _, d in both]
    scatter(0, [dot_tn(p, v) for p, v in zip(probs, values)])
    scatter(3, [dot_nn(p, g) for p, g in zip(probs, cots)])
    scatter(2, [dot_nn(d, q) * scaling for d, q in zip(dscores, queries)])
    scatter(1, [dot_tn(d, k) * scaling for d, k in zip(dscores, keys)])
    key_sums = jnp.concatenate(sums, axis=0)
    norm = jnp.sqrt(jnp.mean(key_sums * key_sums, axis=-1, keepdims=True) + EPSILON)
    centroid_ref[0] = key_sums / norm


def owner(me, got, per_source, head, heads, previous):
    rows, width = got[0].shape
    shapes = [jax.ShapeDtypeStruct((rows, width), BF16)] * (len(got) // 2)
    held = jax.ShapeDtypeStruct((heads, rows // 2 // per_source, HEAD_DIM), F32)
    any_spec = pl.BlockSpec(memory_space=pl.ANY)
    *back, centroids = pl.pallas_call(
        lambda *refs: owner_kernel(*refs, per_source=per_source, sources=len(got)),
        grid=(1,),
        in_specs=[scalar_spec()] + [whole(g) for g in got] + [any_spec] * len(previous),
        out_specs=[whole(s) for s in shapes]
        + [pl.BlockSpec((1,) + held.shape[1:], lambda i: (head, 0, 0))],
        out_shape=shapes + [held],
        input_output_aliases={1 + len(got) + n: len(shapes) + n for n in range(len(previous))},
        name="owner",
        compiler_params=PARAMS,
    )(me, *got, *previous)
    return back, centroids


def unpack_kernel(me_ref, flat_ref, *refs, chunks):
    home_refs = refs[:chunks]
    width = home_refs[0].shape[1]
    out_refs = refs[-(width // HEAD_DIM) :]
    tokens = flat_ref.shape[1]
    rows = home_refs[0].shape[0] // 2
    wide = jnp.broadcast_to(flat_ref[:1, :], (HEAD_DIM, tokens)).T.astype(jnp.int32)[:, :rows]
    lane = iota((tokens, rows), 1)
    chosen = jnp.concatenate(
        [
            jnp.where(wide - (me_ref[0, 0] ^ m) * rows == lane, 1.0, 0.0).astype(BF16)
            for m in range(chunks)
        ],
        axis=1,
    )
    home = jnp.concatenate(
        [ref[m % 2 * rows : (m % 2 + 1) * rows] for m, ref in enumerate(home_refs)], axis=0
    )
    moved = dot_nn(chosen, home).astype(BF16)
    for n, out_ref in enumerate(out_refs):
        out_ref[...] = moved[:, n * HEAD_DIM : (n + 1) * HEAD_DIM]


def unpack(me, flat, home, head, heads, previous):
    tokens = flat.shape[1]
    outs = home[0].shape[1] // HEAD_DIM
    any_spec = pl.BlockSpec(memory_space=pl.ANY)
    return pl.pallas_call(
        lambda *refs: unpack_kernel(*refs, chunks=len(home)),
        grid=(1,),
        in_specs=[scalar_spec(), whole(flat)] + [whole(h) for h in home] + [any_spec] * len(previous),
        out_specs=[pl.BlockSpec((tokens, HEAD_DIM), lambda i: (0, head))] * outs,
        out_shape=[jax.ShapeDtypeStruct((tokens, heads * HEAD_DIM), BF16)] * outs,
        input_output_aliases={2 + len(home) + n: n for n in range(len(previous))},
        name="unpack",
        compiler_params=PARAMS,
    )(me, flat, *home, *previous)


def swap(array, mask):
    size = lax.axis_size("ctx")
    return lax.ppermute(array, "ctx", [(i, i ^ mask) for i in range(size)])


def send_far(pairs):
    far = [swap(pair, 2 * p) for p, pair in list(enumerate(pairs))[:0:-1]]
    return pairs[:1] + far[::-1]


def send_near(pairs):
    near = [swap(pairs[0], 1)]
    near += [swap(pair, 1) for pair in pairs[1:]]
    return [array for both in zip(pairs, near) for array in both]


def shift_rows(array, sign):
    count, lanes = array.shape
    row = iota((count, lanes), 0)
    step = 1
    while step < count:
        rolled = pltpu.roll(array, step if sign > 0 else lanes - step, 1)
        array = jnp.where((row & step) != 0, rolled, array)
        step *= 2
    return array


def local_kernel(
    first_ref,
    bias_ref,
    q_ref,
    k_ref,
    v_ref,
    g_ref,
    pk_ref,
    pv_ref,
    nq_ref,
    nk_ref,
    nv_ref,
    ng_ref,
    out_ref,
    dq_ref,
    dk_ref,
    dv_ref,
    part_ref,
):
    tokens, dim = q_ref.shape
    scaling = dim ** (-0.5)
    count = tokens // WINDOW
    size = (WINDOW, WINDOW)
    early = iota(size, 1) < iota(size, 0)
    bias = shift_rows(jnp.broadcast_to(bias_ref[...], size), 1)
    bias_first = jnp.where(early & (first_ref[0, 0] > 0), NEG, bias)
    spots = [slice(b * WINDOW, (b + 1) * WINDOW) for b in range(count)]
    queries = [q_ref[s] for s in spots] + [nq_ref[...]]
    cots = [g_ref[s] for s in spots] + [ng_ref[...]]
    keys = [pk_ref[...]] + [k_ref[s] for s in spots] + [nk_ref[...]]
    values = [pv_ref[...]] + [v_ref[s] for s in spots] + [nv_ref[...]]
    scores = [
        jnp.where(early, dot_nt(keys[b], queries[b]), dot_nt(keys[b + 1], queries[b])) * scaling
        + (bias if b else bias_first)
        for b in range(count + 1)
    ]
    dprobs = [
        jnp.where(early, dot_nt(values[b], cots[b]), dot_nt(values[b + 1], cots[b]))
        for b in range(count + 1)
    ]
    both = [softmax_down(s, d) for s, d in zip(scores, dprobs)]
    total = both[0][1]
    for b in range(1, count):
        total = total + both[b][1]
    zero = jnp.zeros(size, F32)
    probs = [
        (jnp.where(early, p, zero).astype(BF16), jnp.where(early, zero, p).astype(BF16)) for p, _ in both
    ]
    dscores = [
        (jnp.where(early, d, zero).astype(BF16), jnp.where(early, zero, d).astype(BF16)) for _, d in both
    ]
    for b, s in enumerate(spots):
        out_ref[s] = (dot_tn(probs[b][0], values[b]) + dot_tn(probs[b][1], values[b + 1])).astype(BF16)
        dv_ref[s] = (dot_nn(probs[b][1], cots[b]) + dot_nn(probs[b + 1][0], cots[b + 1])).astype(BF16)
        dk = dot_nn(dscores[b][1], queries[b]) + dot_nn(dscores[b + 1][0], queries[b + 1])
        dk_ref[s] = (dk * scaling).astype(BF16)
        dq = dot_tn(dscores[b][0], keys[b]) + dot_tn(dscores[b][1], keys[b + 1])
        dq_ref[s] = (dq * scaling).astype(BF16)
    part = jnp.sum(shift_rows(total, -1), axis=0, keepdims=True)
    part = jnp.broadcast_to(part[None], part_ref.shape)

    @pl.when(pl.program_id(0) == 0)
    def _():
        part_ref[...] = part

    @pl.when(pl.program_id(0) > 0)
    def _():
        part_ref[...] += part


def local(first, rel_bias, own, behind, ahead, copies):
    tokens, columns = own[0].shape
    heads = columns // HEAD_DIM
    column = pl.BlockSpec((tokens, HEAD_DIM), lambda h: (0, h))

    def halo(n):
        return pl.BlockSpec((WINDOW, HEAD_DIM), lambda h: (0, n * heads + h))

    part = jax.ShapeDtypeStruct((copies, 8, WINDOW), F32)
    return pl.pallas_call(
        local_kernel,
        grid=(heads,),
        in_specs=[scalar_spec(), whole(rel_bias)]
        + [column] * 4
        + [halo(0), halo(1), halo(0), halo(1), halo(2), halo(3)],
        out_specs=[column] * 4 + [whole(part)],
        out_shape=[jax.ShapeDtypeStruct((tokens, columns), BF16)] * 4 + [part],
        name="local",
        compiler_params=PARAMS,
    )(first, rel_bias, *own, behind, behind, ahead, ahead, ahead, ahead)


def shards(
    routed_q,
    routed_k,
    routed_v,
    routed_grad,
    local_q,
    local_k,
    local_v,
    local_grad,
    clusters,
    cluster_slot,
    rel_bias,
):
    ctx_size = lax.axis_size("ctx")
    device_count = ctx_size * lax.axis_size("head")
    tokens = routed_q.shape[0]
    per_source = 2 * tokens // cluster_slot.shape[1]

    heads = cluster_slot.shape[0]
    me = lax.axis_index("ctx").reshape(1, 1)
    in_hbm = lambda arrays: tuple(pltpu.with_memory_space_constraint(a, pltpu.HBM) for a in arrays)
    routed = in_hbm((routed_q, routed_k, routed_v, routed_grad))
    own = in_hbm((local_q, local_k, local_v, local_grad))
    clusters, cluster_slot = in_hbm((clusters, cluster_slot))

    flats, got = [], []
    for head in range(heads):
        ends = own if head == heads - 1 else ()
        flat, chunks = pack(
            me, clusters, cluster_slot, routed, head, ctx_size, per_source, ends
        )
        flats.append(flat)
        if ends:
            *chunks, lead, tail = chunks
        got.append(send_far(chunks))
    got = [send_near(pairs) for pairs in got]

    behind = lax.ppermute(tail, "ctx", [(i, i + 1) for i in range(ctx_size - 1)])
    ahead = lax.ppermute(lead, "ctx", [(i + 1, i) for i in range(ctx_size - 1)])

    centroids, home = (), []
    for head in range(heads):
        back, *centroids = owner(me, got[head], per_source, head, heads, centroids)
        home.append(send_far(back))
    home = [send_near(pairs) for pairs in home]
    (centroids,) = centroids

    first = (lax.axis_index("ctx") == 0).astype(jnp.int32).reshape(1, 1)
    local_out, local_dq, local_dk, local_dv, part = local(
        first, rel_bias.reshape(1, WINDOW), own, behind, ahead, device_count
    )
    parts = lax.all_to_all(part, ("ctx", "head"), 0, 0, tiled=True)
    bias_grad = jnp.sum(parts[:, 0], axis=0)

    columns = ()
    for head in range(heads):
        columns = unpack(me, flats[head], home[head], head, heads, columns)
    routed_out, routed_dq, routed_dk, routed_dv = columns
    return (
        routed_out,
        routed_dq,
        routed_dk,
        routed_dv,
        centroids,
        local_out,
        local_dq,
        local_dk,
        local_dv,
        bias_grad,
    )


def solution(mesh):
    return jax.shard_map(
        shards,
        mesh=mesh,
        in_specs=(
            P("ctx", "head"),
            P("ctx", "head"),
            P("ctx", "head"),
            P("ctx", "head"),
            P("ctx", "head"),
            P("ctx", "head"),
            P("ctx", "head"),
            P("ctx", "head"),
            P("head", "ctx"),
            P("head", None),
            P(),
        ),
        out_specs=(
            P("ctx", "head"),
            P("ctx", "head"),
            P("ctx", "head"),
            P("ctx", "head"),
            P("head", "ctx", None),
            P("ctx", "head"),
            P("ctx", "head"),
            P("ctx", "head"),
            P("ctx", "head"),
            P(),
        ),
        check_vma=False,
    )
```

```python
import jax
import jax.numpy as jnp
from jax import lax
from jax.experimental import pallas as pl
from jax.experimental.pallas import tpu as pltpu
from jax.sharding import PartitionSpec as P


HEAD_DIM = 128
WINDOW = 128

NEG = -1e30
EPSILON = 1e-06
EMPTY = 64.0
EMPTY_LEVEL = 32.0

PARAMS = pltpu.CompilerParams(vmem_limit_bytes=16 << 20)

F32 = jnp.float32
BF16 = jnp.bfloat16


def dot_nn(a, b):
    return lax.dot_general(a, b, (((1,), (0,)), ((), ())), preferred_element_type=F32)


def dot_nt(a, b):
    return lax.dot_general(a, b, (((1,), (1,)), ((), ())), preferred_element_type=F32)


def dot_tn(a, b):
    return lax.dot_general(a, b, (((0,), (0,)), ((), ())), preferred_element_type=F32)


def iota(shape, dim):
    return lax.broadcasted_iota(jnp.int32, shape, dim)


def softmax_down(scores, dprobs):
    exponent = jnp.exp(scores - jnp.max(scores, axis=0, keepdims=True))
    probs = exponent * (1.0 / jnp.sum(exponent, axis=0, keepdims=True))
    weighted = probs * dprobs
    return probs, weighted - probs * jnp.sum(weighted, axis=0, keepdims=True)


def pack_kernel(me_ref, ids_ref, slots_ref, q_ref, k_ref, v_ref, g_ref, *refs, head, per_source, halo):
    halo_refs, (flat_ref, *out_refs) = refs[:halo], refs[halo:]
    if halo:
        *out_refs, tail_ref = out_refs
        for n, ref in enumerate(halo_refs):
            tail_ref[:, n * ref.shape[1] : (n + 1) * ref.shape[1]] = ref[...]
    ids = ids_ref[head : head + 1, :]
    tokens = ids.shape[1]
    clusters = slots_ref.shape[1]
    rows = out_refs[0].shape[0] // 2
    member = iota((clusters, tokens), 0) == ids
    member_low = jnp.where(member, 1.0, 0.0).astype(BF16)
    earlier = jnp.where(iota((tokens, tokens), 0) < iota((tokens, tokens), 1), 1.0, 0.0).astype(BF16)
    before = dot_nn(member_low, earlier)
    rank = jnp.sum(jnp.where(member, before, 0.0), axis=0, keepdims=True)
    slots = jnp.broadcast_to(slots_ref[head : head + 1, :], (8, clusters)).astype(F32).astype(BF16)
    flat = dot_nn(slots, member_low)[:1] * per_source + rank
    flat_ref[...] = jnp.broadcast_to(flat, flat_ref.shape)
    where_to = flat.astype(jnp.int32)
    data = jnp.concatenate([q_ref[...], k_ref[...], v_ref[...], g_ref[...]], axis=1)
    dim = k_ref.shape[1]
    me = me_ref[0, 0]
    slot = iota((rows, tokens), 0)
    chosen = [jnp.where(slot == where_to - (me ^ m) * rows, 1.0, 0.0) for m in range(2 * len(out_refs))]
    moved = dot_nn(jnp.concatenate([c.astype(BF16) for c in chosen], axis=0), data)
    first_col = iota((rows, dim), 1) == 0
    for m in range(2 * len(out_refs)):
        out_ref = out_refs[m // 2]
        at = slice(m % 2 * rows, (m % 2 + 1) * rows)
        part = moved[m * rows : (m + 1) * rows]
        filled = jnp.sum(chosen[m], axis=1, keepdims=True) > 0.5
        marked = jnp.where(first_col & ~filled, EMPTY, part[:, dim : 2 * dim])
        out_ref[at, :dim] = part[:, :dim].astype(BF16)
        out_ref[at, dim : 2 * dim] = marked.astype(BF16)
        out_ref[at, 2 * dim :] = part[:, 2 * dim :].astype(BF16)


def scalar_spec():
    return pl.BlockSpec((1, 1), lambda *_: (0, 0), memory_space=pltpu.SMEM)


def whole(array):
    return pl.BlockSpec(array.shape, lambda *_: (0,) * array.ndim)


def pack(me, ids, slots, arrays, head, dests, per_source, own):
    tokens = arrays[0].shape[0]
    clusters = slots.shape[1]
    rows = clusters * per_source // dests
    width = len(arrays) * HEAD_DIM
    column = pl.BlockSpec((tokens, HEAD_DIM), lambda i: (0, head))
    shapes = [jax.ShapeDtypeStruct((8, tokens), F32)]
    shapes += [jax.ShapeDtypeStruct((2 * rows, width), BF16)] * (dests // 2)
    operands, specs = [], []
    if own:
        columns = own[0].shape[1]
        operands = [*own]
        specs = [pl.BlockSpec((WINDOW, columns), lambda i: (tokens // WINDOW - 1, 0))] * len(own)
        shapes += [jax.ShapeDtypeStruct((WINDOW, len(own) * columns), BF16)]
    flat, *chunks = pl.pallas_call(
        lambda *refs: pack_kernel(*refs, head=head, per_source=per_source, halo=len(operands)),
        grid=(1,),
        in_specs=[scalar_spec(), whole(ids), whole(slots)] + [column] * 4 + specs,
        out_specs=[whole(s) for s in shapes],
        out_shape=shapes,
        name="pack",
        compiler_params=PARAMS,
    )(me, ids, slots, *arrays, *operands)
    return flat, chunks


def owner_kernel(me_ref, *refs, per_source, sources):
    got_refs = refs[:sources]
    out_refs = refs[-sources // 2 - 1 : -1]
    centroid_ref = refs[-1]
    dim = HEAD_DIM
    capacity = sources * per_source
    rows = got_refs[0].shape[0] // 2
    clusters = rows // per_source
    key = iota((capacity, capacity), 0)
    query = iota((capacity, capacity), 1)
    base = me_ref[0, 0] * per_source
    causal = (key ^ base) <= (query ^ base)
    diagonal = key == query
    first_col = iota((capacity, dim), 1) == 0
    scaling = dim ** (-0.5)
    spots = [c * per_source for c in range(clusters)]

    def gathered(part):
        at = slice(part * dim, (part + 1) * dim)
        return [
            jnp.concatenate(
                [ref[m % 2 * rows + spot : m % 2 * rows + spot + per_source, at] for m, ref in enumerate(got_refs)],
                axis=0,
            )
            for spot in spots
        ]

    def scatter(part, results):
        at = slice(part * dim, (part + 1) * dim)
        for spot, result in zip(spots, results):
            for m in range(sources):
                to = m % 2 * rows + spot
                out_refs[m // 2][to : to + per_source, at] = result[
                    m * per_source : (m + 1) * per_source
                ].astype(BF16)

    queries, keys, values, cots = (gathered(part) for part in range(4))
    scores, sums = [], []
    for q, k in zip(queries, keys):
        wide = k.astype(F32)
        live = wide[:, :1] < EMPTY_LEVEL
        scores.append(jnp.where((live & causal) | diagonal, dot_nt(k, q) * scaling, NEG))
        sums.append(jnp.sum(jnp.where(first_col & ~live, 0.0, wide), axis=0, keepdims=True))
    dprobs = [dot_nt(v, g) for v, g in zip(values, cots)]
    both = [softmax_down(s, d) for s, d in zip(scores, dprobs)]
    probs = [p.astype(BF16) for p, _ in both]
    dscores = [d.astype(BF16) for _, d in both]
    scatter(0, [dot_tn(p, v) for p, v in zip(probs, values)])
    scatter(3, [dot_nn(p, g) for p, g in zip(probs, cots)])
    scatter(2, [dot_nn(d, q) * scaling for d, q in zip(dscores, queries)])
    scatter(1, [dot_tn(d, k) * scaling for d, k in zip(dscores, keys)])
    key_sums = jnp.concatenate(sums, axis=0)
    norm = jnp.sqrt(jnp.mean(key_sums * key_sums, axis=-1, keepdims=True) + EPSILON)
    centroid_ref[0] = key_sums / norm


def owner(me, got, per_source, head, heads, previous):
    rows, width = got[0].shape
    shapes = [jax.ShapeDtypeStruct((rows, width), BF16)] * (len(got) // 2)
    held = jax.ShapeDtypeStruct((heads, rows // 2 // per_source, HEAD_DIM), F32)
    any_spec = pl.BlockSpec(memory_space=pl.ANY)
    *back, centroids = pl.pallas_call(
        lambda *refs: owner_kernel(*refs, per_source=per_source, sources=len(got)),
        grid=(1,),
        in_specs=[scalar_spec()] + [whole(g) for g in got] + [any_spec] * len(previous),
        out_specs=[whole(s) for s in shapes]
        + [pl.BlockSpec((1,) + held.shape[1:], lambda i: (head, 0, 0))],
        out_shape=shapes + [held],
        input_output_aliases={1 + len(got) + n: len(shapes) + n for n in range(len(previous))},
        name="owner",
        compiler_params=PARAMS,
    )(me, *got, *previous)
    return back, centroids


def unpack_kernel(me_ref, flat_ref, *refs, chunks):
    home_refs = refs[:chunks]
    width = home_refs[0].shape[1]
    out_refs = refs[-(width // HEAD_DIM) :]
    tokens = flat_ref.shape[1]
    rows = home_refs[0].shape[0] // 2
    wide = jnp.broadcast_to(flat_ref[:1, :], (HEAD_DIM, tokens)).T.astype(jnp.int32)[:, :rows]
    lane = iota((tokens, rows), 1)
    chosen = jnp.concatenate(
        [
            jnp.where(wide - (me_ref[0, 0] ^ m) * rows == lane, 1.0, 0.0).astype(BF16)
            for m in range(chunks)
        ],
        axis=1,
    )
    home = jnp.concatenate(
        [ref[m % 2 * rows : (m % 2 + 1) * rows] for m, ref in enumerate(home_refs)], axis=0
    )
    moved = dot_nn(chosen, home).astype(BF16)
    for n, out_ref in enumerate(out_refs):
        out_ref[...] = moved[:, n * HEAD_DIM : (n + 1) * HEAD_DIM]


def unpack(me, flat, home, head, heads, previous):
    tokens = flat.shape[1]
    outs = home[0].shape[1] // HEAD_DIM
    any_spec = pl.BlockSpec(memory_space=pl.ANY)
    return pl.pallas_call(
        lambda *refs: unpack_kernel(*refs, chunks=len(home)),
        grid=(1,),
        in_specs=[scalar_spec(), whole(flat)] + [whole(h) for h in home] + [any_spec] * len(previous),
        out_specs=[pl.BlockSpec((tokens, HEAD_DIM), lambda i: (0, head))] * outs,
        out_shape=[jax.ShapeDtypeStruct((tokens, heads * HEAD_DIM), BF16)] * outs,
        input_output_aliases={2 + len(home) + n: n for n in range(len(previous))},
        name="unpack",
        compiler_params=PARAMS,
    )(me, flat, *home, *previous)


def swap(array, mask):
    size = lax.axis_size("ctx")
    return lax.ppermute(array, "ctx", [(i, i ^ mask) for i in range(size)])


def send_far(pairs):
    far = [swap(pair, 2 * p) for p, pair in list(enumerate(pairs))[:0:-1]]
    return pairs[:1] + far[::-1]


def send_near(pairs):
    near = [swap(pairs[0], 1)]
    near += [swap(pair, 1) for pair in pairs[1:]]
    return [array for both in zip(pairs, near) for array in both]


def shift_rows(array, sign):
    count, lanes = array.shape
    row = iota((count, lanes), 0)
    step = 1
    while step < count:
        rolled = pltpu.roll(array, step if sign > 0 else lanes - step, 1)
        array = jnp.where((row & step) != 0, rolled, array)
        step *= 2
    return array


def local_kernel(
    first_ref,
    bias_ref,
    q_ref,
    k_ref,
    v_ref,
    g_ref,
    pk_ref,
    pv_ref,
    out_ref,
    dq_ref,
    dk_ref,
    dv_ref,
    edge_ref,
    rest_ref,
    part_ref,
):
    tokens, dim = q_ref.shape
    scaling = dim ** (-0.5)
    count = tokens // WINDOW
    size = (WINDOW, WINDOW)
    early = iota(size, 1) < iota(size, 0)
    bias = shift_rows(jnp.broadcast_to(bias_ref[...], size), 1)
    bias_first = jnp.where(early & (first_ref[0, 0] > 0), NEG, bias)
    spots = [slice(b * WINDOW, (b + 1) * WINDOW) for b in range(count)]
    queries = [q_ref[s] for s in spots]
    cots = [g_ref[s] for s in spots]
    keys = [pk_ref[...]] + [k_ref[s] for s in spots]
    values = [pv_ref[...]] + [v_ref[s] for s in spots]
    scores = [
        jnp.where(early, dot_nt(keys[b], queries[b]), dot_nt(keys[b + 1], queries[b])) * scaling
        + (bias if b else bias_first)
        for b in range(count)
    ]
    dprobs = [
        jnp.where(early, dot_nt(values[b], cots[b]), dot_nt(values[b + 1], cots[b]))
        for b in range(count)
    ]
    both = [softmax_down(s, d) for s, d in zip(scores, dprobs)]
    total = both[0][1]
    for b in range(1, count):
        total = total + both[b][1]
    zero = jnp.zeros(size, F32)
    probs = [
        (jnp.where(early, p, zero).astype(BF16), jnp.where(early, zero, p).astype(BF16)) for p, _ in both
    ]
    dscores = [
        (jnp.where(early, d, zero).astype(BF16), jnp.where(early, zero, d).astype(BF16)) for _, d in both
    ]
    for b, s in enumerate(spots):
        out_ref[s] = (dot_tn(probs[b][0], values[b]) + dot_tn(probs[b][1], values[b + 1])).astype(BF16)
        dq = dot_tn(dscores[b][0], keys[b]) + dot_tn(dscores[b][1], keys[b + 1])
        dq_ref[s] = (dq * scaling).astype(BF16)
        dk = dot_nn(dscores[b][1], queries[b])
        dv = dot_nn(probs[b][1], cots[b])
        if b + 1 < count:
            dk_ref[s] = ((dk + dot_nn(dscores[b + 1][0], queries[b + 1])) * scaling).astype(BF16)
            dv_ref[s] = (dv + dot_nn(probs[b + 1][0], cots[b + 1])).astype(BF16)
        else:
            rest_ref[:, :dim] = dk * scaling
            rest_ref[:, dim:] = dv
    edge_ref[:, :dim] = (dot_nn(dscores[0][0], queries[0]) * scaling).astype(BF16)
    edge_ref[:, dim:] = dot_nn(probs[0][0], cots[0]).astype(BF16)
    part = jnp.sum(shift_rows(total, -1), axis=0, keepdims=True)
    part = jnp.broadcast_to(part[None], part_ref.shape)

    @pl.when(pl.program_id(0) == 0)
    def _():
        part_ref[...] = part

    @pl.when(pl.program_id(0) > 0)
    def _():
        part_ref[...] += part


def local(first, rel_bias, own, behind, copies):
    tokens, columns = own[0].shape
    heads = columns // HEAD_DIM
    column = pl.BlockSpec((tokens, HEAD_DIM), lambda h: (0, h))
    both = pl.BlockSpec((WINDOW, 2 * HEAD_DIM), lambda h: (0, h))

    def halo(n):
        return pl.BlockSpec((WINDOW, HEAD_DIM), lambda h: (0, n * heads + h))

    part = jax.ShapeDtypeStruct((copies, 8, WINDOW), F32)
    return pl.pallas_call(
        local_kernel,
        grid=(heads,),
        in_specs=[scalar_spec(), whole(rel_bias)] + [column] * 4 + [halo(0), halo(1)],
        out_specs=[column] * 4 + [both, both, whole(part)],
        out_shape=[jax.ShapeDtypeStruct((tokens, columns), BF16)] * 4
        + [jax.ShapeDtypeStruct((WINDOW, 2 * columns), kind) for kind in (BF16, F32)]
        + [part],
        name="local",
        compiler_params=PARAMS,
    )(first, rel_bias, *own, behind, behind)


def finish_kernel(edge_ref, rest_ref, parts_ref, *refs):
    dk_ref, dv_ref, bias_ref = refs[-3:]
    total = rest_ref[...] + edge_ref[...].astype(F32)
    for head in range(dk_ref.shape[1] // HEAD_DIM):
        to = slice(head * HEAD_DIM, (head + 1) * HEAD_DIM)
        at = 2 * head * HEAD_DIM
        dk_ref[:, to] = total[:, at : at + HEAD_DIM].astype(BF16)
        dv_ref[:, to] = total[:, at + HEAD_DIM : at + 2 * HEAD_DIM].astype(BF16)
    bias_ref[...] = jnp.sum(parts_ref[...], axis=0)[:1]


def finish(edge, rest, parts, grads):
    tokens, columns = grads[0].shape
    any_spec = pl.BlockSpec(memory_space=pl.ANY)
    bias = jax.ShapeDtypeStruct((1, WINDOW), F32)
    return pl.pallas_call(
        finish_kernel,
        grid=(1,),
        in_specs=[whole(edge), whole(rest), whole(parts)] + [any_spec] * 2,
        out_specs=[pl.BlockSpec((WINDOW, columns), lambda i: (tokens // WINDOW - 1, 0))] * 2
        + [whole(bias)],
        out_shape=[jax.ShapeDtypeStruct(g.shape, g.dtype) for g in grads] + [bias],
        input_output_aliases={3: 0, 4: 1},
        name="finish",
        compiler_params=PARAMS,
    )(edge, rest, parts, *grads)


def shards(
    routed_q,
    routed_k,
    routed_v,
    routed_grad,
    local_q,
    local_k,
    local_v,
    local_grad,
    clusters,
    cluster_slot,
    rel_bias,
):
    ctx_size = lax.axis_size("ctx")
    device_count = ctx_size * lax.axis_size("head")
    tokens = routed_q.shape[0]
    per_source = 2 * tokens // cluster_slot.shape[1]

    heads = cluster_slot.shape[0]
    me = lax.axis_index("ctx").reshape(1, 1)
    in_hbm = lambda arrays: tuple(pltpu.with_memory_space_constraint(a, pltpu.HBM) for a in arrays)
    routed = in_hbm((routed_q, routed_k, routed_v, routed_grad))
    own = in_hbm((local_q, local_k, local_v, local_grad))
    clusters, cluster_slot = in_hbm((clusters, cluster_slot))

    flats, got = [], []
    for head in range(heads):
        ends = own[1:3] if head == heads - 1 else ()
        flat, chunks = pack(me, clusters, cluster_slot, routed, head, ctx_size, per_source, ends)
        flats.append(flat)
        if ends:
            *chunks, tail = chunks
        got.append(send_far(chunks))
    got = [send_near(pairs) for pairs in got]

    behind = lax.ppermute(tail, "ctx", [(i, i + 1) for i in range(ctx_size - 1)])

    centroids, home = (), []
    for head in range(heads):
        back, *centroids = owner(me, got[head], per_source, head, heads, centroids)
        home.append(send_far(back))
    home = [send_near(pairs) for pairs in home]
    (centroids,) = centroids

    first = (lax.axis_index("ctx") == 0).astype(jnp.int32).reshape(1, 1)
    local_out, local_dq, *local_grads, edge, rest, part = local(
        first, rel_bias.reshape(1, WINDOW), own, behind, device_count
    )
    edge = lax.ppermute(edge, "ctx", [(i + 1, i) for i in range(ctx_size - 1)])
    parts = lax.all_to_all(part, ("ctx", "head"), 0, 0, tiled=True)
    local_dk, local_dv, bias_grad = finish(edge, rest, parts, local_grads)

    columns = ()
    for head in range(heads):
        columns = unpack(me, flats[head], home[head], head, heads, columns)
    routed_out, routed_dq, routed_dk, routed_dv = columns
    return (
        routed_out,
        routed_dq,
        routed_dk,
        routed_dv,
        centroids,
        local_out,
        local_dq,
        local_dk,
        local_dv,
        bias_grad[0],
    )


def solution(mesh):
    return jax.shard_map(
        shards,
        mesh=mesh,
        in_specs=(
            P("ctx", "head"),
            P("ctx", "head"),
            P("ctx", "head"),
            P("ctx", "head"),
            P("ctx", "head"),
            P("ctx", "head"),
            P("ctx", "head"),
            P("ctx", "head"),
            P("head", "ctx"),
            P("head", None),
            P(),
        ),
        out_specs=(
            P("ctx", "head"),
            P("ctx", "head"),
            P("ctx", "head"),
            P("ctx", "head"),
            P("head", "ctx", None),
            P("ctx", "head"),
            P("ctx", "head"),
            P("ctx", "head"),
            P("ctx", "head"),
            P(),
        ),
        check_vma=False,
    )
```

```python
import jax
import jax.numpy as jnp
from jax import lax
from jax.experimental import pallas as pl
from jax.experimental.pallas import tpu as pltpu
from jax.sharding import PartitionSpec as P


HEAD_DIM = 128
WINDOW = 128

NEG = -1e30
EPSILON = 1e-06
EMPTY = 64.0
EMPTY_LEVEL = 32.0

PARAMS = pltpu.CompilerParams(vmem_limit_bytes=16 << 20)

F32 = jnp.float32
BF16 = jnp.bfloat16


def dot_nn(a, b):
    return lax.dot_general(a, b, (((1,), (0,)), ((), ())), preferred_element_type=F32)


def dot_nt(a, b):
    return lax.dot_general(a, b, (((1,), (1,)), ((), ())), preferred_element_type=F32)


def dot_tn(a, b):
    return lax.dot_general(a, b, (((0,), (0,)), ((), ())), preferred_element_type=F32)


def iota(shape, dim):
    return lax.broadcasted_iota(jnp.int32, shape, dim)


def softmax_down(scores, dprobs):
    exponent = jnp.exp(scores - jnp.max(scores, axis=0, keepdims=True))
    probs = exponent * (1.0 / jnp.sum(exponent, axis=0, keepdims=True))
    weighted = probs * dprobs
    return probs, weighted - probs * jnp.sum(weighted, axis=0, keepdims=True)


def pack_kernel(me_ref, ids_ref, slots_ref, q_ref, k_ref, v_ref, g_ref, *refs, head, per_source, halo):
    halo_refs, (flat_ref, *out_refs) = refs[:halo], refs[halo:]
    if halo:
        *out_refs, tail_ref = out_refs
        for n, ref in enumerate(halo_refs):
            tail_ref[:, n * ref.shape[1] : (n + 1) * ref.shape[1]] = ref[...]
    ids = ids_ref[head : head + 1, :]
    tokens = ids.shape[1]
    clusters = slots_ref.shape[1]
    rows = out_refs[0].shape[0] // 2
    member = iota((clusters, tokens), 0) == ids
    member_low = jnp.where(member, 1.0, 0.0).astype(BF16)
    earlier = jnp.where(iota((tokens, tokens), 0) < iota((tokens, tokens), 1), 1.0, 0.0).astype(BF16)
    before = dot_nn(member_low, earlier)
    rank = jnp.sum(jnp.where(member, before, 0.0), axis=0, keepdims=True)
    slots = jnp.broadcast_to(slots_ref[head : head + 1, :], (8, clusters)).astype(F32).astype(BF16)
    flat = dot_nn(slots, member_low)[:1] * per_source + rank
    flat_ref[...] = jnp.broadcast_to(flat, flat_ref.shape)
    where_to = flat.astype(jnp.int32)
    data = jnp.concatenate([q_ref[...], k_ref[...], v_ref[...], g_ref[...]], axis=1)
    dim = k_ref.shape[1]
    me = me_ref[0, 0]
    slot = iota((rows, tokens), 0)
    chosen = [jnp.where(slot == where_to - (me ^ m) * rows, 1.0, 0.0) for m in range(2 * len(out_refs))]
    moved = dot_nn(jnp.concatenate([c.astype(BF16) for c in chosen], axis=0), data)
    first_col = iota((rows, dim), 1) == 0
    for m in range(2 * len(out_refs)):
        out_ref = out_refs[m // 2]
        at = slice(m % 2 * rows, (m % 2 + 1) * rows)
        part = moved[m * rows : (m + 1) * rows]
        filled = jnp.sum(chosen[m], axis=1, keepdims=True) > 0.5
        marked = jnp.where(first_col & ~filled, EMPTY, part[:, dim : 2 * dim])
        out_ref[at, :dim] = part[:, :dim].astype(BF16)
        out_ref[at, dim : 2 * dim] = marked.astype(BF16)
        out_ref[at, 2 * dim :] = part[:, 2 * dim :].astype(BF16)


def scalar_spec():
    return pl.BlockSpec((1, 1), lambda *_: (0, 0), memory_space=pltpu.SMEM)


def whole(array):
    return pl.BlockSpec(array.shape, lambda *_: (0,) * array.ndim)


def halves(arrays):
    rows, width = arrays[0].shape
    return [pl.BlockSpec((rows // 2, width), lambda i, m=m: (m % 2, 0)) for m in range(len(arrays))]


def pack(me, ids, slots, arrays, head, dests, per_source, own):
    tokens = arrays[0].shape[0]
    clusters = slots.shape[1]
    rows = clusters * per_source // dests
    width = len(arrays) * HEAD_DIM
    column = pl.BlockSpec((tokens, HEAD_DIM), lambda i: (0, head))
    shapes = [jax.ShapeDtypeStruct((8, tokens), F32)]
    shapes += [jax.ShapeDtypeStruct((2 * rows, width), BF16)] * (dests // 2)
    operands, specs = [], []
    if own:
        columns = own[0].shape[1]
        operands = [*own]
        specs = [pl.BlockSpec((WINDOW, columns), lambda i: (tokens // WINDOW - 1, 0))] * len(own)
        shapes += [jax.ShapeDtypeStruct((WINDOW, len(own) * columns), BF16)]
    flat, *chunks = pl.pallas_call(
        lambda *refs: pack_kernel(*refs, head=head, per_source=per_source, halo=len(operands)),
        grid=(1,),
        in_specs=[scalar_spec(), whole(ids), whole(slots)] + [column] * 4 + specs,
        out_specs=[whole(s) for s in shapes],
        out_shape=shapes,
        name="pack",
        compiler_params=PARAMS,
    )(me, ids, slots, *arrays, *operands)
    return flat, chunks


def owner_kernel(me_ref, *refs, per_source, sources):
    got_refs = refs[:sources]
    out_refs = refs[-sources // 2 - 1 : -1]
    centroid_ref = refs[-1]
    dim = HEAD_DIM
    capacity = sources * per_source
    rows = got_refs[0].shape[0]
    clusters = rows // per_source
    key = iota((capacity, capacity), 0)
    query = iota((capacity, capacity), 1)
    base = me_ref[0, 0] * per_source
    causal = (key ^ base) <= (query ^ base)
    diagonal = key == query
    first_col = iota((capacity, dim), 1) == 0
    scaling = dim ** (-0.5)
    spots = [c * per_source for c in range(clusters)]

    def gathered(part):
        at = slice(part * dim, (part + 1) * dim)
        return [
            jnp.concatenate(
                [ref[spot : spot + per_source, at] for ref in got_refs], axis=0
            )
            for spot in spots
        ]

    def scatter(part, results):
        at = slice(part * dim, (part + 1) * dim)
        for spot, result in zip(spots, results):
            for m in range(sources):
                to = m % 2 * rows + spot
                out_refs[m // 2][to : to + per_source, at] = result[
                    m * per_source : (m + 1) * per_source
                ].astype(BF16)

    queries, keys, values, cots = (gathered(part) for part in range(4))
    scores, sums = [], []
    for q, k in zip(queries, keys):
        wide = k.astype(F32)
        live = wide[:, :1] < EMPTY_LEVEL
        scores.append(jnp.where((live & causal) | diagonal, dot_nt(k, q) * scaling, NEG))
        sums.append(jnp.sum(jnp.where(first_col & ~live, 0.0, wide), axis=0, keepdims=True))
    dprobs = [dot_nt(v, g) for v, g in zip(values, cots)]
    both = [softmax_down(s, d) for s, d in zip(scores, dprobs)]
    probs = [p.astype(BF16) for p, _ in both]
    dscores = [d.astype(BF16) for _, d in both]
    scatter(0, [dot_tn(p, v) for p, v in zip(probs, values)])
    scatter(3, [dot_nn(p, g) for p, g in zip(probs, cots)])
    scatter(2, [dot_nn(d, q) * scaling for d, q in zip(dscores, queries)])
    scatter(1, [dot_tn(d, k) * scaling for d, k in zip(dscores, keys)])
    key_sums = jnp.concatenate(sums, axis=0)
    norm = jnp.sqrt(jnp.mean(key_sums * key_sums, axis=-1, keepdims=True) + EPSILON)
    centroid_ref[0] = key_sums / norm


def owner(me, got, per_source, head, heads, previous):
    rows, width = got[0].shape
    shapes = [jax.ShapeDtypeStruct((rows, width), BF16)] * (len(got) // 2)
    held = jax.ShapeDtypeStruct((heads, rows // 2 // per_source, HEAD_DIM), F32)
    any_spec = pl.BlockSpec(memory_space=pl.ANY)
    *back, centroids = pl.pallas_call(
        lambda *refs: owner_kernel(*refs, per_source=per_source, sources=len(got)),
        grid=(1,),
        in_specs=[scalar_spec()] + halves(got) + [any_spec] * len(previous),
        out_specs=[whole(s) for s in shapes]
        + [pl.BlockSpec((1,) + held.shape[1:], lambda i: (head, 0, 0))],
        out_shape=shapes + [held],
        input_output_aliases={1 + len(got) + n: len(shapes) + n for n in range(len(previous))},
        name="owner",
        compiler_params=PARAMS,
    )(me, *got, *previous)
    return back, centroids


def unpack_kernel(me_ref, flat_ref, *refs, chunks):
    home_refs = refs[:chunks]
    width = home_refs[0].shape[1]
    out_refs = refs[-(width // HEAD_DIM) :]
    tokens = flat_ref.shape[1]
    rows = home_refs[0].shape[0]
    wide = jnp.broadcast_to(flat_ref[:1, :], (HEAD_DIM, tokens)).T.astype(jnp.int32)[:, :rows]
    lane = iota((tokens, rows), 1)
    chosen = jnp.concatenate(
        [
            jnp.where(wide - (me_ref[0, 0] ^ m) * rows == lane, 1.0, 0.0).astype(BF16)
            for m in range(chunks)
        ],
        axis=1,
    )
    home = jnp.concatenate([ref[...] for ref in home_refs], axis=0)
    moved = dot_nn(chosen, home).astype(BF16)
    for n, out_ref in enumerate(out_refs):
        out_ref[...] = moved[:, n * HEAD_DIM : (n + 1) * HEAD_DIM]


def unpack(me, flat, home, head, heads, previous):
    tokens = flat.shape[1]
    outs = home[0].shape[1] // HEAD_DIM
    any_spec = pl.BlockSpec(memory_space=pl.ANY)
    return pl.pallas_call(
        lambda *refs: unpack_kernel(*refs, chunks=len(home)),
        grid=(1,),
        in_specs=[scalar_spec(), whole(flat)] + halves(home) + [any_spec] * len(previous),
        out_specs=[pl.BlockSpec((tokens, HEAD_DIM), lambda i: (0, head))] * outs,
        out_shape=[jax.ShapeDtypeStruct((tokens, heads * HEAD_DIM), BF16)] * outs,
        input_output_aliases={2 + len(home) + n: n for n in range(len(previous))},
        name="unpack",
        compiler_params=PARAMS,
    )(me, flat, *home, *previous)


def swap(array, mask):
    size = lax.axis_size("ctx")
    return lax.ppermute(array, "ctx", [(i, i ^ mask) for i in range(size)])


def send_far(pairs):
    far = [swap(pair, 2 * p) for p, pair in list(enumerate(pairs))[:0:-1]]
    return pairs[:1] + far[::-1]


def send_near(pairs):
    near = [swap(pairs[0], 1)]
    near += [swap(pair, 1) for pair in pairs[1:]]
    return [array for both in zip(pairs, near) for array in both]


def shift_rows(array, sign):
    count, lanes = array.shape
    row = iota((count, lanes), 0)
    step = 1
    while step < count:
        rolled = pltpu.roll(array, step if sign > 0 else lanes - step, 1)
        array = jnp.where((row & step) != 0, rolled, array)
        step *= 2
    return array


def local_kernel(
    first_ref,
    bias_ref,
    q_ref,
    k_ref,
    v_ref,
    g_ref,
    pk_ref,
    pv_ref,
    out_ref,
    dq_ref,
    dk_ref,
    dv_ref,
    edge_ref,
    rest_ref,
    part_ref,
):
    tokens, dim = q_ref.shape
    scaling = dim ** (-0.5)
    count = tokens // WINDOW
    size = (WINDOW, WINDOW)
    early = iota(size, 1) < iota(size, 0)
    bias = shift_rows(jnp.broadcast_to(bias_ref[...], size), 1)
    bias_first = jnp.where(early & (first_ref[0, 0] > 0), NEG, bias)
    spots = [slice(b * WINDOW, (b + 1) * WINDOW) for b in range(count)]
    queries = [q_ref[s] for s in spots]
    cots = [g_ref[s] for s in spots]
    keys = [pk_ref[...]] + [k_ref[s] for s in spots]
    values = [pv_ref[...]] + [v_ref[s] for s in spots]
    scores = [
        jnp.where(early, dot_nt(keys[b], queries[b]), dot_nt(keys[b + 1], queries[b])) * scaling
        + (bias if b else bias_first)
        for b in range(count)
    ]
    dprobs = [
        jnp.where(early, dot_nt(values[b], cots[b]), dot_nt(values[b + 1], cots[b]))
        for b in range(count)
    ]
    both = [softmax_down(s, d) for s, d in zip(scores, dprobs)]
    total = both[0][1]
    for b in range(1, count):
        total = total + both[b][1]
    zero = jnp.zeros(size, F32)
    probs = [
        (jnp.where(early, p, zero).astype(BF16), jnp.where(early, zero, p).astype(BF16)) for p, _ in both
    ]
    dscores = [
        (jnp.where(early, d, zero).astype(BF16), jnp.where(early, zero, d).astype(BF16)) for _, d in both
    ]
    for b, s in enumerate(spots):
        out_ref[s] = (dot_tn(probs[b][0], values[b]) + dot_tn(probs[b][1], values[b + 1])).astype(BF16)
        dq = dot_tn(dscores[b][0], keys[b]) + dot_tn(dscores[b][1], keys[b + 1])
        dq_ref[s] = (dq * scaling).astype(BF16)
        dk = dot_nn(dscores[b][1], queries[b])
        dv = dot_nn(probs[b][1], cots[b])
        if b + 1 < count:
            dk_ref[s] = ((dk + dot_nn(dscores[b + 1][0], queries[b + 1])) * scaling).astype(BF16)
            dv_ref[s] = (dv + dot_nn(probs[b + 1][0], cots[b + 1])).astype(BF16)
        else:
            rest_ref[:, :dim] = dk * scaling
            rest_ref[:, dim:] = dv
    edge_ref[:, :dim] = (dot_nn(dscores[0][0], queries[0]) * scaling).astype(BF16)
    edge_ref[:, dim:] = dot_nn(probs[0][0], cots[0]).astype(BF16)
    part = jnp.sum(shift_rows(total, -1), axis=0, keepdims=True)
    part = jnp.broadcast_to(part[None], part_ref.shape)

    @pl.when(pl.program_id(0) == 0)
    def _():
        part_ref[...] = part

    @pl.when(pl.program_id(0) > 0)
    def _():
        part_ref[...] += part


def local(first, rel_bias, own, behind, copies):
    tokens, columns = own[0].shape
    heads = columns // HEAD_DIM
    column = pl.BlockSpec((tokens, HEAD_DIM), lambda h: (0, h))
    both = pl.BlockSpec((WINDOW, 2 * HEAD_DIM), lambda h: (0, h))

    def halo(n):
        return pl.BlockSpec((WINDOW, HEAD_DIM), lambda h: (0, n * heads + h))

    part = jax.ShapeDtypeStruct((copies, 8, WINDOW), F32)
    return pl.pallas_call(
        local_kernel,
        grid=(heads,),
        in_specs=[scalar_spec(), whole(rel_bias)] + [column] * 4 + [halo(0), halo(1)],
        out_specs=[column] * 4 + [both, both, whole(part)],
        out_shape=[jax.ShapeDtypeStruct((tokens, columns), BF16)] * 4
        + [jax.ShapeDtypeStruct((WINDOW, 2 * columns), kind) for kind in (BF16, F32)]
        + [part],
        name="local",
        compiler_params=PARAMS,
    )(first, rel_bias, *own, behind, behind)


def finish_kernel(edge_ref, rest_ref, parts_ref, *refs):
    dk_ref, dv_ref, bias_ref = refs[-3:]
    total = rest_ref[...] + edge_ref[...].astype(F32)
    for head in range(dk_ref.shape[1] // HEAD_DIM):
        to = slice(head * HEAD_DIM, (head + 1) * HEAD_DIM)
        at = 2 * head * HEAD_DIM
        dk_ref[:, to] = total[:, at : at + HEAD_DIM].astype(BF16)
        dv_ref[:, to] = total[:, at + HEAD_DIM : at + 2 * HEAD_DIM].astype(BF16)
    bias_ref[...] = jnp.sum(parts_ref[...], axis=0)[:1]


def finish(edge, rest, parts, grads):
    tokens, columns = grads[0].shape
    any_spec = pl.BlockSpec(memory_space=pl.ANY)
    bias = jax.ShapeDtypeStruct((1, WINDOW), F32)
    return pl.pallas_call(
        finish_kernel,
        grid=(1,),
        in_specs=[whole(edge), whole(rest), whole(parts)] + [any_spec] * 2,
        out_specs=[pl.BlockSpec((WINDOW, columns), lambda i: (tokens // WINDOW - 1, 0))] * 2
        + [whole(bias)],
        out_shape=[jax.ShapeDtypeStruct(g.shape, g.dtype) for g in grads] + [bias],
        input_output_aliases={3: 0, 4: 1},
        name="finish",
        compiler_params=PARAMS,
    )(edge, rest, parts, *grads)


def shards(
    routed_q,
    routed_k,
    routed_v,
    routed_grad,
    local_q,
    local_k,
    local_v,
    local_grad,
    clusters,
    cluster_slot,
    rel_bias,
):
    ctx_size = lax.axis_size("ctx")
    device_count = ctx_size * lax.axis_size("head")
    tokens = routed_q.shape[0]
    per_source = 2 * tokens // cluster_slot.shape[1]

    heads = cluster_slot.shape[0]
    me = lax.axis_index("ctx").reshape(1, 1)
    in_hbm = lambda arrays: tuple(pltpu.with_memory_space_constraint(a, pltpu.HBM) for a in arrays)
    routed = in_hbm((routed_q, routed_k, routed_v, routed_grad))
    own = in_hbm((local_q, local_k, local_v, local_grad))
    clusters, cluster_slot, bias_row = in_hbm((clusters, cluster_slot, rel_bias.reshape(1, WINDOW)))

    flats, got = [], []
    for head in range(heads):
        ends = own[1:3] if head == heads - 1 else ()
        flat, chunks = pack(me, clusters, cluster_slot, routed, head, ctx_size, per_source, ends)
        flats.append(flat)
        if ends:
            *chunks, tail = chunks
        got.append(send_far(chunks))
    got = [send_near(pairs) for pairs in got]

    behind = lax.ppermute(tail, "ctx", [(i, i + 1) for i in range(ctx_size - 1)])

    centroids, home = (), []
    for head in range(heads):
        back, *centroids = owner(me, got[head], per_source, head, heads, centroids)
        home.append(send_far(back))
    home = [send_near(pairs) for pairs in home]
    (centroids,) = centroids

    first = (lax.axis_index("ctx") == 0).astype(jnp.int32).reshape(1, 1)
    local_out, local_dq, *local_grads, edge, rest, part = local(
        first, bias_row, own, behind, device_count
    )
    edge = lax.ppermute(edge, "ctx", [(i + 1, i) for i in range(ctx_size - 1)])
    parts = lax.all_to_all(part, ("ctx", "head"), 0, 0, tiled=True)
    local_dk, local_dv, bias_grad = finish(edge, rest, parts, local_grads)

    columns = ()
    for head in range(heads):
        columns = unpack(me, flats[head], home[head], head, heads, columns)
    routed_out, routed_dq, routed_dk, routed_dv = columns
    return (
        routed_out,
        routed_dq,
        routed_dk,
        routed_dv,
        centroids,
        local_out,
        local_dq,
        local_dk,
        local_dv,
        bias_grad[0],
    )


def solution(mesh):
    return jax.shard_map(
        shards,
        mesh=mesh,
        in_specs=(
            P("ctx", "head"),
            P("ctx", "head"),
            P("ctx", "head"),
            P("ctx", "head"),
            P("ctx", "head"),
            P("ctx", "head"),
            P("ctx", "head"),
            P("ctx", "head"),
            P("head", "ctx"),
            P("head", None),
            P(),
        ),
        out_specs=(
            P("ctx", "head"),
            P("ctx", "head"),
            P("ctx", "head"),
            P("ctx", "head"),
            P("head", "ctx", None),
            P("ctx", "head"),
            P("ctx", "head"),
            P("ctx", "head"),
            P("ctx", "head"),
            P(),
        ),
        check_vma=False,
    )
```
